32 devices in a mesh: rep: 16 (over z, x, core), shard: 2 (over y).
Axes of the slice: x: 2, y: 2, z: 4, core: 2. Of those that a mesh axis runs over, the one named last changes fastest.
Arguments:
- square_grads: bfloat16 [16, 2, 2, 896, 896], P('rep', 'shard'), may hold values from -0.59765625 to 0.59765625
- narrow_grads: bfloat16 [16, 2, 2, 896, 128], P('rep', 'shard'), may hold values from -0.59765625 to 0.59765625
- galore_bases: bfloat16 [2, 896, 256], replicated, may hold values from -0.1875 to 0.1875
- square_first: float32 [256, 2, 896], P('shard'), may hold values from -3 to 3
- square_second: float32 [256, 2, 896], P('shard'), may hold values from 0.25 to 2.5
- narrow_first: float32 [2, 896, 128], P(None, 'shard'), may hold values from -3 to 3
- narrow_second: float32 [2, 896, 128], P(None, 'shard'), may hold values from 0.25 to 2.5
Outputs:
- square_update: bfloat16 [2, 896, 896], replicated
- narrow_update: bfloat16 [2, 896, 128], replicated
- new_square_first: float32 [256, 2, 896], P('shard')
- new_square_second: float32 [256, 2, 896], P('shard')
- new_narrow_first: float32 [2, 896, 128], P(None, 'shard')
- new_narrow_second: float32 [2, 896, 128], P(None, 'shard')
The draws below stay inside these ranges and needn't reach their ends.
All inputs are finite; a program needn't handle non-finite values.
Results may differ from the reference program's by a relative error of at most 0.005.
Values may be sent and summed in bfloat16 or wider, within the bound.
A program may use at most 64 MiB of HBM per device.

```python
import math
import jax
import jax.numpy as jnp
from jax import lax

D = 896
KV = 128
R = 256
STEP = 1000
N_REP = 16
N_SHARD = 2


def block_scale(key, shape, cuts, low, largest):
    def one(position, parts):
        steps = jax.random.uniform(jax.random.fold_in(jax.random.fold_in(key, 6), position), (parts,), jnp.float32, low / len(cuts), largest / len(cuts))
        return jnp.repeat(jnp.exp(steps), shape[position] // parts).reshape((-1,) + (1,) * (len(shape) - position - 1))

    factor_of = one(*cuts[0])
    for cut in cuts[1:]:
        factor_of = factor_of * one(*cut)
    return factor_of


def noise(own_key, dims, spread, limit, split=(), kind=jnp.bfloat16):
    entries = jax.random.normal(own_key, dims, jnp.float32) * spread
    if len(split) > 0:
        entries = block_scale(own_key, dims, split, -0.22, 0.18) * entries
    return jnp.clip(entries, min=-limit, max=limit).astype(kind)


def setup_inputs(seed: int = 0) -> dict:
    keys = jax.random.split(jax.random.key(seed), 8)
    square_grads = noise(keys[0], (N_REP, N_SHARD, 2, D, D), 0.1, 0.59765625, ((0, 16), (1, 2)))
    narrow_grads = noise(keys[1], (N_REP, N_SHARD, 2, D, KV), 0.1, 0.59765625, ((0, 16), (1, 2)))
    galore_bases = noise(keys[2], (2, D, R), D ** -0.5, 0.1875)
    square_first = noise(keys[3], (R, 2, D), 0.5, 3.0, ((0, 2),), jnp.float32)
    square_second = jnp.clip(jnp.exp(math.log(2.5) - 2.3025851 * jax.random.uniform(keys[4], (R, 2, D), jnp.float32) ** block_scale(keys[4], (R, 2, D), ((0, 2),), -0.2, 0.2)), 0.25, 2.5)
    narrow_first = noise(keys[5], (2, D, KV), 0.5, 3.0, ((1, 2),), jnp.float32)
    narrow_second = jnp.clip(jnp.exp(math.log(2.5) - 2.3025851 * jax.random.uniform(keys[6], (2, D, KV), jnp.float32) ** block_scale(keys[6], (2, D, KV), ((1, 2),), -0.2, 0.2)), 0.25, 2.5)
    return dict(square_grads=square_grads, narrow_grads=narrow_grads, galore_bases=galore_bases, square_first=square_first, square_second=square_second, narrow_first=narrow_first, narrow_second=narrow_second)


beta_one = 0.9
beta_two = 0.999
epsilon = 1e-08

def device_sum(gradients):
    flat = gradients.reshape((-1,) + gradients.shape[2:])

    def add_one(running, block_piece):
        return (running + block_piece.astype(jnp.float32), None)
    summed, _ = lax.scan(add_one, jnp.zeros(flat.shape[1:], jnp.float32), flat)
    return summed

def adam_update(gradient, moment_one, moment_two):
    first_new = beta_one * moment_one + (1.0 - beta_one) * gradient
    second_new = beta_two * moment_two + (1.0 - beta_two) * gradient * gradient
    correct_one = 1.0 - beta_one ** STEP
    correct_two = 1.0 - beta_two ** STEP
    direction = first_new / correct_one / (jnp.sqrt(second_new / correct_two) + epsilon)
    return (direction, first_new, second_new)

def reference(square_grads, narrow_grads, galore_bases, square_first, square_second, narrow_first, narrow_second):
    square_sum = device_sum(square_grads)
    narrow_sum = device_sum(narrow_grads)
    bases_wide = galore_bases.astype(jnp.float32)
    projected = jnp.einsum('imr,imn->rin', bases_wide, square_sum, precision=lax.Precision.HIGHEST)
    square_dir, new_square_first, new_square_second = adam_update(projected, square_first, square_second)
    narrow_dir, new_narrow_first, new_narrow_second = adam_update(narrow_sum, narrow_first, narrow_second)
    square_update = jnp.einsum('imr,rin->imn', bases_wide, square_dir, precision=lax.Precision.HIGHEST).astype(jnp.bfloat16)
    narrow_update = narrow_dir.astype(jnp.bfloat16)
    return (square_update, narrow_update, new_square_first, new_square_second, new_narrow_first, new_narrow_second)
```

```python
import functools

import jax
import jax.numpy as jnp
from jax import lax
from jax.experimental import pallas as pl
from jax.experimental.pallas import tpu as pltpu
from jax.sharding import PartitionSpec as P

STEP = 1000


beta_one = 0.9
beta_two = 0.999
epsilon = 1e-08
MESH = pl.DeviceIdType.MESH
CORES = 2
MIDDLE = 2
TILES = 4


def adam_update(gradient, moment_one, moment_two):
    first_new = beta_one * moment_one + (1.0 - beta_one) * gradient
    second_new = beta_two * moment_two + (1.0 - beta_two) * gradient * gradient
    correct_one = 1.0 - beta_one**STEP
    correct_two = 1.0 - beta_two**STEP
    direction = first_new * (1.0 / correct_one) / (
        jnp.sqrt(second_new * (1.0 / correct_two)) + epsilon
    )
    return (direction, first_new, second_new)


def plain_exchange(square, narrow, bases, square_first, square_second, narrow_first, narrow_second):
    partial = jnp.einsum("imr,imn->rin", bases, square, preferred_element_type=jnp.float32)

    def total(value, axis):
        part = lax.psum_scatter(
            value.astype(jnp.bfloat16), "shard", scatter_dimension=axis, tiled=True
        )
        return lax.psum(part, "rep").astype(jnp.float32)

    square_dir, new_square_first, new_square_second = adam_update(
        total(partial, 0), square_first, square_second
    )
    narrow_dir, new_narrow_first, new_narrow_second = adam_update(
        total(narrow, 1), narrow_first, narrow_second
    )
    directions = lax.all_gather(square_dir.astype(jnp.bfloat16), "shard", axis=0, tiled=True)
    square_update = jnp.einsum(
        "imr,rin->imn", bases, directions, preferred_element_type=jnp.float32
    ).astype(jnp.bfloat16)
    narrow_update = lax.all_gather(narrow_dir.astype(jnp.bfloat16), "shard", axis=1, tiled=True)
    return (
        square_update,
        narrow_update,
        new_square_first,
        new_square_second,
        new_narrow_first,
        new_narrow_second,
    )


class Stream:
    def __init__(self, part, own, refs, far_by_shard):
        self.part, self.own, self.far_by_shard = part, own, far_by_shard
        (
            self.in1,
            self.sum1,
            self.in2,
            self.sum2,
            self.in3,
            self.total,
            self.direction,
            self.one,
            self.two,
            self.one_out,
            self.two_out,
            self.columns,
        ) = refs


def kernel(shards, high, cuts, *refs):
    quads = shards * MIDDLE
    pieces = len(cuts)
    refs = list(refs)

    def take(number):
        taken = refs[:number]
        del refs[:number]
        return taken

    grads_hbm, narrow_hbm, bases_hbm, sq_one_hbm, sq_two_hbm, na_one_hbm, na_two_hbm = take(7)
    directions_out = take(pieces + 1)
    sq_one_out, sq_two_out, na_one_out, na_two_out = take(4)
    grads, bases, narrow, sq_one, sq_two, na_one, na_two = take(7)
    parts = take(pieces)
    buffers = [take(6) for _ in range(pieces + 1)]
    loads, sends, recvs = take(3)

    me_rep = lax.axis_index("rep")
    s = lax.axis_index("shard")
    c = lax.rem(me_rep, CORES)
    m = lax.rem(me_rep // CORES, MIDDLE)
    h = me_rep // (CORES * MIDDLE)
    q = s * MIDDLE + m

    def device(hh, mm, cc, ss):
        return ((hh * MIDDLE + mm) * CORES + cc, ss)

    core_peer = device(h, m, 1 - c, s)
    middle_peer = device(h, 1 - m, c, s)
    quad_peers = []
    for d in range(1, quads):
        qq = lax.rem(q + d, quads)
        quad_peers.append(device(h, lax.rem(qq, MIDDLE), c, qq // MIDDLE))
    high_peers = []
    for e in range(1, high):
        hh = lax.rem(h + e, high)
        high_peers.append((hh, device(hh, m, c, s)))
    shard_peers = []
    for f in range(1, shards):
        shard_peers.append(device(h, m, c, lax.rem(s + f, shards)))

    barrier = pltpu.get_barrier_semaphore()
    everyone = [core_peer] + quad_peers + [peer for _, peer in high_peers]
    for peer in everyone:
        pl.semaphore_signal(barrier, inc=1, device_id=peer, device_id_type=MESH)

    loading = []

    def load(source, target):
        copy = pltpu.make_async_copy(source, target, loads.at[len(loading)])
        copy.start()
        loading.append(copy)
        return copy

    needed = {}
    for turn, i in enumerate((1 - c, c)):
        needed[turn, "bases"] = load(bases_hbm.at[i], bases.at[i])
        for k, cut in enumerate(cuts):
            needed[turn, k] = load(grads_hbm.at[i, :, cut], grads.at[i, :, cut])
    needed["narrow"] = load(narrow_hbm.at[c], narrow)
    moments = [load(na_one_hbm, na_one), load(na_two_hbm, na_two)]
    for i in range(CORES):
        moments.append(load(sq_one_hbm.at[:, i, :], sq_one.at[i]))
        moments.append(load(sq_two_hbm.at[:, i, :], sq_two.at[i]))

    waited = set()

    def ready(key):
        if key not in waited:
            waited.add(key)
            needed[key].wait()

    def moments_ready():
        while moments:
            moments.pop(0).wait()

    pending = []

    def send(source, target, peer):
        at = len(pending)
        copy = pltpu.make_async_remote_copy(
            src_ref=source,
            dst_ref=target,
            send_sem=sends.at[at],
            recv_sem=recvs.at[at],
            device_id=peer,
            device_id_type=MESH,
        )
        copy.start()
        pending.append(copy)
        return copy

    def wide(value):
        return value.astype(jnp.float32)

    def adam_group(st, cc, mm):
        shape = st.total.shape[2:]
        rows = shape[0] * shape[1]
        at = pl.ds(pl.multiple_of(mm * rows, rows), rows)
        gradient = wide(st.total[cc, mm]).reshape(rows, shape[2])
        direction, one, two = adam_update(
            gradient, st.one[cc, at, st.columns], st.two[cc, at, st.columns]
        )
        st.direction[cc, s, mm] = direction.astype(jnp.bfloat16).reshape(shape)
        st.one_out[cc, at, st.columns] = one
        st.two_out[cc, at, st.columns] = two

    def exchange(st):
        order = list(range(1, quads)) + [0]
        first = {}
        there = st.part(1 - c)
        if not waited.intersection(("barrier",)):
            waited.add("barrier")
            pl.semaphore_wait(barrier, len(everyone))
        for d in order:
            first[d] = send(there.at[lax.rem(q + d, quads)], st.in1.at[d], core_peer)
        yield
        here = st.own()
        second = []
        for d in order:
            first[d].wait_recv()
            st.sum1[d] = (wide(here[lax.rem(q + d, quads)]) + wide(st.in1[d])).astype(jnp.bfloat16)
            if d > 0:
                second.append(send(st.sum1.at[d], st.in2.at[d - 1], quad_peers[d - 1]))
        yield
        total = wide(st.sum1[0])
        for d, copy in enumerate(second):
            copy.wait_recv()
            total = total + wide(st.in2[d])
        st.sum2[...] = total.astype(jnp.bfloat16)
        third = []
        for e, (hh, peer) in enumerate(high_peers):
            third.append(send(st.sum2.at[hh], st.in3.at[e], peer))
        yield
        total = wide(st.sum2[h])
        for e, copy in enumerate(third):
            copy.wait_recv()
            total = total + wide(st.in3[e])
        st.total[c, m, h] = total.astype(jnp.bfloat16)
        mine = st.total.at[c, m, h]
        back = [send(mine, mine, peer) for _, peer in high_peers]
        yield
        for copy in back:
            copy.wait_recv()
        mine = st.total.at[c, m]
        total_middle = send(mine, mine, middle_peer)
        moments_ready()
        adam_group(st, c, m)
        mine = st.direction.at[c, s, m]
        near = [send(mine, mine, peer) for peer in shard_peers]
        total_core = send(st.total.at[c, m], st.total.at[c, m], core_peer)
        yield
        total_middle.wait_recv()
        mine = st.total.at[c, 1 - m]
        total_core_far = send(mine, mine, core_peer)
        adam_group(st, c, 1 - m)
        far = []
        if st.far_by_shard:
            mine = st.direction.at[c, s, 1 - m]
            far = [send(mine, mine, peer) for peer in shard_peers]
        total_core.wait_recv()
        adam_group(st, 1 - c, m)
        yield
        last = []
        for f, copy in enumerate(near):
            copy.wait_recv()
            came = st.direction.at[c, lax.rem(s + shards - 1 - f, shards), m]
            if not st.far_by_shard:
                far.append(send(came, came, middle_peer))
            last.append(send(came, came, core_peer))
        total_core_far.wait_recv()
        adam_group(st, 1 - c, 1 - m)
        yield
        for f, copy in enumerate(far):
            copy.wait_recv()
            came = st.direction.at[c, lax.rem(s + shards - 1 - f, shards), 1 - m]
            last.append(send(came, came, core_peer))
        yield
        for copy in last:
            copy.wait_recv()

    def square_part(k):
        def project(turn, i):
            ready((turn, "bases"))
            ready((turn, k))
            part = lax.dot_general(
                bases[i],
                grads[i, :, cuts[k]],
                (((0,), (0,)), ((), ())),
                preferred_element_type=jnp.float32,
            )
            parts[k][i] = part.astype(jnp.bfloat16).reshape(parts[k].shape[1:])
            return parts[k].at[i]

        return (lambda i: project(0, i)), (lambda: project(1, c))

    def narrow_own():
        ready("narrow")
        return narrow

    whole = slice(None)
    streams = [
        Stream(
            lambda i: narrow_hbm.at[i],
            narrow_own,
            buffers[pieces]
            + [directions_out[pieces], na_one, na_two, na_one_out, na_two_out, whole],
            False,
        )
    ]
    for k, cut in enumerate(cuts):
        there, own = square_part(k)
        streams.append(
            Stream(
                there,
                own,
                buffers[k] + [directions_out[k], sq_one, sq_two, sq_one_out, sq_two_out, cut],
                True,
            )
        )
    running = [exchange(st) for st in streams]
    while running:
        running = [one for one in running if next(one, one) is None]
    for copy in pending:
        copy.wait_send()


def finish(cuts, bases_ref, *refs):
    sq_dir_refs = refs[: len(cuts)]
    na_dir_ref, sq_one_ref, sq_two_ref, na_one_ref, na_two_ref = refs[len(cuts) : len(cuts) + 5]
    update_out, na_update_out, sq_one_out, sq_two_out, na_one_out, na_two_out = refs[-9:-3]
    update, sems, tile_sems = refs[-3:]
    pairs = [(na_dir_ref, na_update_out), (na_one_ref, na_one_out), (na_two_ref, na_two_out)]
    for i in range(CORES):
        pairs.append((sq_one_ref.at[i], sq_one_out.at[:, i, :]))
        pairs.append((sq_two_ref.at[i], sq_two_out.at[:, i, :]))
    copies = [
        pltpu.make_async_copy(source, target, sems.at[k])
        for k, (source, target) in enumerate(pairs)
    ]
    for copy in copies:
        copy.start()
    height = update.shape[1] // TILES
    for i in range(CORES):
        for t in range(TILES):
            rows = pl.ds(t * height, height)
            for cut, sq_dir_ref in zip(cuts, sq_dir_refs):
                update[i, rows, cut] = jnp.dot(
                    bases_ref[i, rows], sq_dir_ref[i], preferred_element_type=jnp.float32
                ).astype(jnp.bfloat16)
            copy = pltpu.make_async_copy(
                update.at[i, rows], update_out.at[i, rows], tile_sems.at[i, t]
            )
            copy.start()
            copies.append(copy)
    for copy in copies:
        copy.wait()


def kernel_exchange(shards, reps, square, narrow, bases, square_first, square_second, narrow_first, narrow_second):
    matrices, width, columns = square.shape
    rank = bases.shape[2]
    high = reps // (CORES * MIDDLE)
    quads = shards * MIDDLE
    bf16, f32 = jnp.bfloat16, jnp.float32
    half = -(-columns // 256) * 128
    cuts = [slice(0, half), slice(half, columns)]
    kinds = [(rank // (quads * high), cut.stop - cut.start) for cut in cuts]
    na = (width // (quads * high), narrow.shape[2])
    kinds.append(na)
    own = (matrices, MIDDLE, high)
    own_square = (matrices, rank // shards, columns)

    buffers = []
    for kind in kinds:
        shapes = [
            (quads, high) + kind,
            (quads, high) + kind,
            (quads - 1, high) + kind,
            (high,) + kind,
            (high - 1,) + kind,
            own + kind,
        ]
        buffers += [pltpu.VMEM(shape, bf16) for shape in shapes]
    copies = len(kinds) * (quads + (quads - 1) + 2 * (high - 1) + 3 + 4 * (shards - 1))
    vmem = pl.BlockSpec(memory_space=pltpu.VMEM)
    anywhere = pl.BlockSpec(memory_space=pl.ANY)
    out = pl.pallas_call(
        functools.partial(kernel, shards, high, cuts),
        out_shape=tuple(
            [jax.ShapeDtypeStruct((matrices, shards, MIDDLE, high) + kind, bf16) for kind in kinds]
            + [jax.ShapeDtypeStruct(own_square, f32)] * 2
            + [jax.ShapeDtypeStruct(narrow_first.shape, f32)] * 2
        ),
        in_specs=[pl.BlockSpec(memory_space=pltpu.HBM)] * 7,
        out_specs=[vmem] * (len(kinds) + 4),
        scratch_shapes=[
            pltpu.VMEM(square.shape, bf16),
            pltpu.VMEM(bases.shape, bf16),
            pltpu.VMEM((quads, high) + na, bf16),
            pltpu.VMEM(own_square, f32),
            pltpu.VMEM(own_square, f32),
            pltpu.VMEM(narrow_first.shape, f32),
            pltpu.VMEM(narrow_first.shape, f32),
        ]
        + [pltpu.VMEM((matrices, quads, high) + kind, bf16) for kind in kinds[:-1]]
        + buffers
        + [
            pltpu.SemaphoreType.DMA((2 * (1 + len(cuts)) + 3 + 2 * matrices,)),
            pltpu.SemaphoreType.DMA((copies,)),
            pltpu.SemaphoreType.DMA((copies,)),
        ],
        compiler_params=pltpu.CompilerParams(
            collective_id=0, has_side_effects=True, vmem_limit_bytes=48 * 1024 * 1024
        ),
        name="galore_exchange",
    )(
        *[pltpu.with_memory_space_constraint(v, pltpu.HBM) for v in (
        square,
        narrow.reshape((matrices, quads, high) + na),
        bases,
        square_first,
        square_second,
        narrow_first,
        narrow_second,
    )])
    *sq_dirs, na_dir, sq_one, sq_two, na_one, na_two = out
    return pl.pallas_call(
        functools.partial(finish, cuts),
        out_shape=(
            jax.ShapeDtypeStruct(square.shape, bf16),
            jax.ShapeDtypeStruct(narrow.shape, bf16),
            jax.ShapeDtypeStruct(square_first.shape, f32),
            jax.ShapeDtypeStruct(square_second.shape, f32),
            jax.ShapeDtypeStruct(narrow_first.shape, f32),
            jax.ShapeDtypeStruct(narrow_second.shape, f32),
        ),
        in_specs=[vmem] * (6 + len(cuts)),
        out_specs=[anywhere] * 6,
        scratch_shapes=[
            pltpu.VMEM(square.shape, bf16),
            pltpu.SemaphoreType.DMA((7,)),
            pltpu.SemaphoreType.DMA((matrices, TILES)),
        ],
        compiler_params=pltpu.CompilerParams(vmem_limit_bytes=24 * 1024 * 1024),
        name="galore_finish",
    )(
        bases,
        *[part.reshape(matrices, rank, -1) for part in sq_dirs],
        na_dir.reshape(narrow.shape),
        sq_one,
        sq_two,
        na_one,
        na_two,
    )


def on_device(square_grads, narrow_grads, galore_bases, *moments):
    shards, reps = lax.axis_size("shard"), lax.axis_size("rep")
    square, narrow = square_grads[0, 0], narrow_grads[0, 0]
    chunks = shards * reps // CORES
    fits = (
        reps % (CORES * MIDDLE) == 0
        and reps > CORES * MIDDLE
        and shards > 1
        and square.shape[0] == CORES
        and square.shape[2] % 128 == 0
        and square.shape[2] > 128
        and galore_bases.shape[2] % (16 * chunks) == 0
        and square.shape[1] % (8 * chunks) == 0
        and square.shape[1] % (16 * TILES) == 0
    )
    run = functools.partial(kernel_exchange, shards, reps) if fits else plain_exchange
    return run(square, narrow, galore_bases, *moments)


def solution(mesh):
    placed = (
        P("rep", "shard", None, None, None),
        P("rep", "shard", None, None, None),
        P(),
        P("shard", None, None),
        P("shard", None, None),
        P(None, "shard", None),
        P(None, "shard", None),
    )
    return jax.shard_map(
        on_device,
        mesh=mesh,
        in_specs=placed,
        out_specs=(
            P(),
            P(),
            P("shard", None, None),
            P("shard", None, None),
            P(None, "shard", None),
            P(None, "shard", None),
        ),
        check_vma=False,
    )
```

```python
import functools
import math

import jax
import jax.numpy as jnp
from jax import lax
from jax.experimental import pallas as pl
from jax.experimental.pallas import tpu as pltpu
from jax.sharding import PartitionSpec as P

STEP = 1000


beta_one = 0.9
beta_two = 0.999
epsilon = 1e-08
MESH = pl.DeviceIdType.MESH
CORES = 2
MIDDLE = 2
SHARDS = 2
PIECES = 3
TILES = 4


def adam_update(gradient, moment_one, moment_two):
    first_new = beta_one * moment_one + (1.0 - beta_one) * gradient
    second_new = beta_two * moment_two + (1.0 - beta_two) * gradient * gradient
    correct_one = 1.0 - beta_one**STEP
    correct_two = 1.0 - beta_two**STEP
    direction = first_new * (1.0 / correct_one) / (
        jnp.sqrt(second_new * (1.0 / correct_two)) + epsilon
    )
    return (direction, first_new, second_new)


def plain_exchange(square, narrow, bases, square_first, square_second, narrow_first, narrow_second):
    partial = jnp.einsum("imr,imn->rin", bases, square, preferred_element_type=jnp.float32)

    def total(value, axis):
        part = lax.psum_scatter(
            value.astype(jnp.bfloat16), "shard", scatter_dimension=axis, tiled=True
        )
        return lax.psum(part, "rep").astype(jnp.float32)

    square_dir, new_square_first, new_square_second = adam_update(
        total(partial, 0), square_first, square_second
    )
    narrow_dir, new_narrow_first, new_narrow_second = adam_update(
        total(narrow, 1), narrow_first, narrow_second
    )
    directions = lax.all_gather(square_dir.astype(jnp.bfloat16), "shard", axis=0, tiled=True)
    square_update = jnp.einsum(
        "imr,rin->imn", bases, directions, preferred_element_type=jnp.float32
    ).astype(jnp.bfloat16)
    narrow_update = lax.all_gather(narrow_dir.astype(jnp.bfloat16), "shard", axis=1, tiled=True)
    return (
        square_update,
        narrow_update,
        new_square_first,
        new_square_second,
        new_narrow_first,
        new_narrow_second,
    )


class Stream:
    def __init__(self, part, own, refs):
        self.part, self.own = part, own
        (
            self.in1,
            self.sum1,
            self.in2,
            self.sum2,
            self.in3,
            self.total,
            self.direction,
            self.one,
            self.two,
            self.one_out,
            self.two_out,
            self.columns,
        ) = refs


def kernel(high, cuts, *refs):
    pieces = len(cuts)
    refs = list(refs)

    def take(number):
        taken = refs[:number]
        del refs[:number]
        return taken

    grads_hbm, narrow_hbm, bases_hbm, sq_one_hbm, sq_two_hbm, na_one_hbm, na_two_hbm = take(7)
    directions_out = take(pieces + 1)
    sq_one_out, sq_two_out, na_one_out, na_two_out = take(4)
    grads, bases, narrow, sq_one, sq_two, na_one, na_two = take(7)
    parts = take(pieces)
    buffers = [take(6) for _ in range(pieces + 1)]
    loads, sends, recvs = take(3)

    me_rep = lax.axis_index("rep")
    s = lax.axis_index("shard")
    c = lax.rem(me_rep, CORES)
    m = lax.rem(me_rep // CORES, MIDDLE)
    h = me_rep // (CORES * MIDDLE)

    def device(hh, mm, cc, ss):
        return ((hh * MIDDLE + mm) * CORES + cc, ss)

    def quad(ss, mm):
        return ss * MIDDLE + mm

    q = quad(s, m)
    core_peer = device(h, m, 1 - c, s)
    middle_peer = device(h, 1 - m, c, s)
    shard_peer = device(h, m, c, 1 - s)
    corner_peer = device(h, 1 - m, c, 1 - s)
    quad_peers = [
        (quad(1 - s, 1 - m), corner_peer),
        (quad(s, 1 - m), middle_peer),
        (quad(1 - s, m), shard_peer),
    ]
    high_peers = []
    for e in range(1, high):
        hh = lax.rem(h + e, high)
        high_peers.append((hh, device(hh, m, c, s)))

    barrier = pltpu.get_barrier_semaphore()
    everyone = [core_peer] + [peer for _, peer in high_peers + quad_peers]
    for peer in everyone:
        pl.semaphore_signal(barrier, inc=1, device_id=peer, device_id_type=MESH)

    loading = []

    def load(source, target):
        copy = pltpu.make_async_copy(source, target, loads.at[len(loading)])
        copy.start()
        loading.append(copy)
        return copy

    needed = {}
    for turn, i in enumerate((1 - c, c)):
        needed[turn, "bases"] = load(bases_hbm.at[i], bases.at[i])
        for k, cut in enumerate(cuts):
            needed[turn, k] = load(grads_hbm.at[i, :, cut], grads.at[i, :, cut])
    needed["narrow"] = load(narrow_hbm.at[c], narrow)
    moments = [load(na_one_hbm, na_one), load(na_two_hbm, na_two)]
    for i in range(CORES):
        moments.append(load(sq_one_hbm.at[:, i, :], sq_one.at[i]))
        moments.append(load(sq_two_hbm.at[:, i, :], sq_two.at[i]))

    waited = set()

    def ready(key):
        if key not in waited:
            waited.add(key)
            needed[key].wait()

    def moments_ready():
        while moments:
            moments.pop(0).wait()

    def everyone_ready():
        if "barrier" not in waited:
            waited.add("barrier")
            pl.semaphore_wait(barrier, len(everyone))

    pending = []

    def send(source, target, peer):
        at = len(pending)
        copy = pltpu.make_async_remote_copy(
            src_ref=source,
            dst_ref=target,
            send_sem=sends.at[at],
            recv_sem=recvs.at[at],
            device_id=peer,
            device_id_type=MESH,
        )
        copy.start()
        pending.append(copy)
        return copy

    def wide(value):
        return value.astype(jnp.float32)

    def adam(st, cc, mm, hh=None):
        where = (cc, mm) if hh is None else (cc, mm, hh)
        shape = st.total.shape[len(where) :]
        rows = math.prod(shape[:-1])
        first = mm * rows if hh is None else (mm * high + hh) * rows
        at = pl.ds(pl.multiple_of(first, 8), rows)
        gradient = wide(st.total[where]).reshape(rows, shape[-1])
        direction, one, two = adam_update(
            gradient, st.one[cc, at, st.columns], st.two[cc, at, st.columns]
        )
        st.direction[(cc, s) + where[1:]] = direction.astype(jnp.bfloat16).reshape(shape)
        st.one_out[cc, at, st.columns] = one
        st.two_out[cc, at, st.columns] = two

    def added(value, copies, arrivals):
        total = wide(value)
        for k, copy in enumerate(copies):
            copy.wait_recv()
            total = total + wide(arrivals[k])
        return total.astype(jnp.bfloat16)

    def core_sum(st):
        there = st.part(1 - c)
        everyone_ready()
        first = send(there, st.in1, core_peer)
        yield
        here = st.own()
        first.wait_recv()
        st.sum1[...] = (wide(here[...]) + wide(st.in1[...])).astype(jnp.bfloat16)

    def quad_first(st):
        yield from core_sum(st)
        second = [
            send(st.sum1.at[qq], st.in2.at[k], peer) for k, (qq, peer) in enumerate(quad_peers)
        ]
        yield
        st.sum2[...] = added(st.sum1[q], second, st.in2)
        third = [
            send(st.sum2.at[hh], st.in3.at[k], peer) for k, (hh, peer) in enumerate(high_peers)
        ]
        yield
        st.total[c, m, h] = added(st.sum2[h], third, st.in3)
        mine = st.total.at[c, m, h]
        back = [send(mine, mine, peer) for _, peer in high_peers]
        yield
        for copy in back:
            copy.wait_recv()
        mine = st.total.at[c, m]
        total_middle = send(mine, mine, middle_peer)
        moments_ready()
        adam(st, c, m)
        mine = st.direction.at[c, s, m]
        corner = send(mine, mine, corner_peer)
        shard = send(mine, mine, shard_peer)
        mine = st.total.at[c, m]
        last = [send(mine, mine, core_peer)]
        yield
        last.pop().wait_recv()
        adam(st, 1 - c, m)
        yield
        shard.wait_recv()
        came = st.direction.at[c, 1 - s, m]
        last.append(send(came, came, core_peer))
        yield
        total_middle.wait_recv()
        came = st.total.at[c, 1 - m]
        total_core = send(came, came, core_peer)
        adam(st, c, 1 - m)
        yield
        corner.wait_recv()
        came = st.direction.at[c, 1 - s, 1 - m]
        last.append(send(came, came, core_peer))
        yield
        total_core.wait_recv()
        adam(st, 1 - c, 1 - m)
        for copy in last:
            copy.wait_recv()

    def high_first(st):
        yield from core_sum(st)
        second = [
            send(st.sum1.at[:, hh], st.in2.at[k], peer) for k, (hh, peer) in enumerate(high_peers)
        ]
        yield
        st.sum2[...] = added(st.sum1[:, h], second, st.in2)
        third = [
            send(st.sum2.at[qq], st.in3.at[k], peer) for k, (qq, peer) in enumerate(quad_peers)
        ]
        yield
        st.total[c, m, h] = added(st.sum2[q], third, st.in3)
        mine = st.total.at[c, m, h]
        back = [send(mine, mine, middle_peer)]
        moments_ready()
        adam(st, c, m, h)
        mine = st.direction.at[c, s, m, h]
        back.append(send(mine, mine, corner_peer))
        back.append(send(mine, mine, shard_peer))
        yield
        for copy in back:
            copy.wait_recv()
        totals, ours = st.total.at[c, :, h], st.direction.at[c, 1 - s, :, h]
        last = []
        for _, peer in high_peers:
            last.append(send(totals, totals, peer))
            last.append(send(ours, ours, peer))
        adam(st, c, 1 - m, h)
        yield
        for copy in last:
            copy.wait_recv()
        totals, ours = st.total.at[c], st.direction.at[c, 1 - s]
        total_core = send(totals, totals, core_peer)
        direction_core = send(ours, ours, core_peer)
        for hh, _ in high_peers:
            for mm in range(MIDDLE):
                adam(st, c, mm, hh)
        yield
        total_core.wait_recv()
        for mm in range(MIDDLE):
            adam(st, 1 - c, mm)
        direction_core.wait_recv()

    def square_part(k):
        def project(turn, i):
            ready((turn, "bases"))
            ready((turn, k))
            part = lax.dot_general(
                bases[i],
                grads[i, :, cuts[k]],
                (((0,), (0,)), ((), ())),
                preferred_element_type=jnp.float32,
            )
            parts[k][i] = part.astype(jnp.bfloat16).reshape(parts[k].shape[1:])
            return parts[k].at[i]

        return (lambda i: project(0, i)), (lambda: project(1, c))

    def narrow_own():
        ready("narrow")
        return narrow

    running = [
        high_first(
            Stream(
                lambda i: narrow_hbm.at[i],
                narrow_own,
                buffers[pieces]
                + [directions_out[pieces], na_one, na_two, na_one_out, na_two_out, slice(None)],
            )
        )
    ]
    for k, cut in enumerate(cuts):
        there, own = square_part(k)
        running.append(
            quad_first(
                Stream(
                    there,
                    own,
                    buffers[k] + [directions_out[k], sq_one, sq_two, sq_one_out, sq_two_out, cut],
                )
            )
        )
    for at in sequence(pieces):
        next(running[at], None)
    for copy in pending:
        copy.wait_send()


def sequence(pieces):
    square = list(range(1, pieces + 1))
    turns = [0] + square
    turns += [0] + square
    turns += square + [0]
    turns += square[:1] + [0] + square[1:]
    turns += square[:1] + [0] + square[1:]
    turns += square
    turns += square[:1] * 3 + [0]
    for k in square[1:]:
        turns += [k] * 3
    return turns + [0] + square


def finish(cuts, bases_ref, *refs):
    sq_dir_refs = refs[: len(cuts)]
    na_dir_ref, sq_one_ref, sq_two_ref, na_one_ref, na_two_ref = refs[len(cuts) : len(cuts) + 5]
    update_out, na_update_out, sq_one_out, sq_two_out, na_one_out, na_two_out = refs[-9:-3]
    update, sems, tile_sems = refs[-3:]
    pairs = [(na_dir_ref, na_update_out), (na_one_ref, na_one_out), (na_two_ref, na_two_out)]
    for i in range(CORES):
        pairs.append((sq_one_ref.at[i], sq_one_out.at[:, i, :]))
        pairs.append((sq_two_ref.at[i], sq_two_out.at[:, i, :]))
    copies = [
        pltpu.make_async_copy(source, target, sems.at[k])
        for k, (source, target) in enumerate(pairs)
    ]
    for copy in copies:
        copy.start()
    height = update.shape[1] // TILES
    for i in range(CORES):
        for t in range(TILES):
            rows = pl.ds(t * height, height)
            for cut, sq_dir_ref in zip(cuts, sq_dir_refs):
                update[i, rows, cut] = jnp.dot(
                    bases_ref[i, rows], sq_dir_ref[i], preferred_element_type=jnp.float32
                ).astype(jnp.bfloat16)
            copy = pltpu.make_async_copy(
                update.at[i, rows], update_out.at[i, rows], tile_sems.at[i, t]
            )
            copy.start()
            copies.append(copy)
    for copy in copies:
        copy.wait()


def kernel_exchange(reps, square, narrow, bases, square_first, square_second, narrow_first, narrow_second):
    matrices, width, columns = square.shape
    rank = bases.shape[2]
    high = reps // (CORES * MIDDLE)
    shards = SHARDS
    quads = shards * MIDDLE
    bf16, f32 = jnp.bfloat16, jnp.float32
    cuts = []
    while sum(cut.stop - cut.start for cut in cuts) < columns:
        begin = cuts[-1].stop if cuts else 0
        size = -(-(columns - begin) // ((PIECES - len(cuts)) * 128)) * 128
        cuts.append(slice(begin, min(columns, begin + size)))
    kinds = [(rank // (quads * high), cut.stop - cut.start) for cut in cuts]
    na = (width // (quads * high), narrow.shape[2])
    kinds.append(na)
    own = (matrices, MIDDLE, high)
    own_square = (matrices, rank // shards, columns)

    buffers = []
    for kind in kinds:
        inner, outer = (quads, high) if kind is na else (high, quads)
        shapes = [
            (quads, high) + kind,
            (quads, high) + kind,
            (outer - 1, inner) + kind,
            (inner,) + kind,
            (inner - 1,) + kind,
            own + kind,
        ]
        buffers += [pltpu.VMEM(shape, bf16) for shape in shapes]
    copies = len(kinds) * (8 + (quads - 1) + 4 * (high - 1))
    vmem = pl.BlockSpec(memory_space=pltpu.VMEM)
    anywhere = pl.BlockSpec(memory_space=pl.ANY)
    out = pl.pallas_call(
        functools.partial(kernel, high, cuts),
        out_shape=tuple(
            [jax.ShapeDtypeStruct((matrices, shards, MIDDLE, high) + kind, bf16) for kind in kinds]
            + [jax.ShapeDtypeStruct(own_square, f32)] * 2
            + [jax.ShapeDtypeStruct(narrow_first.shape, f32)] * 2
        ),
        in_specs=[pl.BlockSpec(memory_space=pltpu.HBM)] * 7,
        out_specs=[vmem] * (len(kinds) + 4),
        scratch_shapes=[
            pltpu.VMEM(square.shape, bf16),
            pltpu.VMEM(bases.shape, bf16),
            pltpu.VMEM((quads, high) + na, bf16),
            pltpu.VMEM(own_square, f32),
            pltpu.VMEM(own_square, f32),
            pltpu.VMEM(narrow_first.shape, f32),
            pltpu.VMEM(narrow_first.shape, f32),
        ]
        + [pltpu.VMEM((matrices, quads, high) + kind, bf16) for kind in kinds[:-1]]
        + buffers
        + [
            pltpu.SemaphoreType.DMA((2 * (1 + len(cuts)) + 3 + 2 * matrices,)),
            pltpu.SemaphoreType.DMA((copies,)),
            pltpu.SemaphoreType.DMA((copies,)),
        ],
        compiler_params=pltpu.CompilerParams(
            collective_id=0, has_side_effects=True, vmem_limit_bytes=48 * 1024 * 1024
        ),
        name="galore_exchange",
    )(
        *[
            pltpu.with_memory_space_constraint(operand, pltpu.HBM)
            for operand in (
                square,
                narrow.reshape((matrices, quads, high) + na),
                bases,
                square_first,
                square_second,
                narrow_first,
                narrow_second,
            )
        ]
    )
    *sq_dirs, na_dir, sq_one, sq_two, na_one, na_two = out
    return pl.pallas_call(
        functools.partial(finish, cuts),
        out_shape=(
            jax.ShapeDtypeStruct(square.shape, bf16),
            jax.ShapeDtypeStruct(narrow.shape, bf16),
            jax.ShapeDtypeStruct(square_first.shape, f32),
            jax.ShapeDtypeStruct(square_second.shape, f32),
            jax.ShapeDtypeStruct(narrow_first.shape, f32),
            jax.ShapeDtypeStruct(narrow_second.shape, f32),
        ),
        in_specs=[vmem] * (6 + len(cuts)),
        out_specs=[anywhere] * 6,
        scratch_shapes=[
            pltpu.VMEM(square.shape, bf16),
            pltpu.SemaphoreType.DMA((7,)),
            pltpu.SemaphoreType.DMA((matrices, TILES)),
        ],
        compiler_params=pltpu.CompilerParams(vmem_limit_bytes=24 * 1024 * 1024),
        name="galore_finish",
    )(
        bases,
        *[part.reshape(matrices, rank, -1) for part in sq_dirs],
        na_dir.reshape(narrow.shape),
        sq_one,
        sq_two,
        na_one,
        na_two,
    )


def on_device(square_grads, narrow_grads, galore_bases, *moments):
    shards, reps = lax.axis_size("shard"), lax.axis_size("rep")
    square, narrow = square_grads[0, 0], narrow_grads[0, 0]
    chunks = shards * reps // CORES
    fits = (
        reps % (CORES * MIDDLE) == 0
        and reps > CORES * MIDDLE
        and shards == SHARDS
        and square.shape[0] == CORES
        and square.shape[2] % 128 == 0
        and square.shape[2] >= PIECES * 128
        and galore_bases.shape[2] % (16 * chunks) == 0
        and square.shape[1] % (8 * chunks) == 0
        and square.shape[1] % (16 * TILES) == 0
    )
    run = functools.partial(kernel_exchange, reps) if fits else plain_exchange
    return run(square, narrow, galore_bases, *moments)


def solution(mesh):
    placed = (
        P("rep", "shard", None, None, None),
        P("rep", "shard", None, None, None),
        P(),
        P("shard", None, None),
        P("shard", None, None),
        P(None, "shard", None),
        P(None, "shard", None),
    )
    return jax.shard_map(
        on_device,
        mesh=mesh,
        in_specs=placed,
        out_specs=(
            P(),
            P(),
            P("shard", None, None),
            P("shard", None, None),
            P(None, "shard", None),
            P(None, "shard", None),
        ),
        check_vma=False,
    )
```

```python
import functools
import math

import jax
import jax.numpy as jnp
from jax import lax
from jax.experimental import pallas as pl
from jax.experimental.pallas import tpu as pltpu
from jax.sharding import PartitionSpec as P

STEP = 1000


beta_one = 0.9
beta_two = 0.999
epsilon = 1e-08
MESH = pl.DeviceIdType.MESH
CORES = 2
MIDDLE = 2
SHARDS = 2
PIECES = 3
TILES = 4


def adam_update(gradient, moment_one, moment_two):
    first_new = beta_one * moment_one + (1.0 - beta_one) * gradient
    second_new = beta_two * moment_two + (1.0 - beta_two) * gradient * gradient
    correct_one = 1.0 - beta_one**STEP
    correct_two = 1.0 - beta_two**STEP
    direction = first_new * (1.0 / correct_one) / (
        jnp.sqrt(second_new * (1.0 / correct_two)) + epsilon
    )
    return (direction, first_new, second_new)


def plain_exchange(square, narrow, bases, square_first, square_second, narrow_first, narrow_second):
    partial = jnp.einsum("imr,imn->rin", bases, square, preferred_element_type=jnp.float32)

    def total(value, axis):
        part = lax.psum_scatter(
            value.astype(jnp.bfloat16), "shard", scatter_dimension=axis, tiled=True
        )
        return lax.psum(part, "rep").astype(jnp.float32)

    square_dir, new_square_first, new_square_second = adam_update(
        total(partial, 0), square_first, square_second
    )
    narrow_dir, new_narrow_first, new_narrow_second = adam_update(
        total(narrow, 1), narrow_first, narrow_second
    )
    directions = lax.all_gather(square_dir.astype(jnp.bfloat16), "shard", axis=0, tiled=True)
    square_update = jnp.einsum(
        "imr,rin->imn", bases, directions, preferred_element_type=jnp.float32
    ).astype(jnp.bfloat16)
    narrow_update = lax.all_gather(narrow_dir.astype(jnp.bfloat16), "shard", axis=1, tiled=True)
    return (
        square_update,
        narrow_update,
        new_square_first,
        new_square_second,
        new_narrow_first,
        new_narrow_second,
    )


class Stream:
    def __init__(self, theirs, ours, refs):
        self.theirs, self.ours = theirs, ours
        (
            self.in1,
            self.sum1,
            self.in2,
            self.sum2,
            self.in3,
            self.total,
            self.direction,
            self.one,
            self.two,
            self.one_out,
            self.two_out,
            self.columns,
        ) = refs


def kernel(high, cuts, *refs):
    pieces = len(cuts)
    refs = list(refs)

    def take(number):
        taken = refs[:number]
        del refs[:number]
        return taken

    grads_hbm, narrow_hbm, bases_hbm, sq_one_hbm, sq_two_hbm, na_one_hbm, na_two_hbm = take(7)
    directions_out = take(pieces + 1)
    sq_one_out, sq_two_out, na_one_out, na_two_out = take(4)
    grads, bases, narrow, sq_one, sq_two, na_one, na_two = take(7)
    parts = take(pieces)
    buffers = [take(6) for _ in range(pieces + 1)]
    loads, sends, recvs = take(3)

    me_rep = lax.axis_index("rep")
    s = lax.axis_index("shard")
    c = lax.rem(me_rep, CORES)
    m = lax.rem(me_rep // CORES, MIDDLE)
    h = me_rep // (CORES * MIDDLE)

    def device(hh, mm, cc, ss):
        return ((hh * MIDDLE + mm) * CORES + cc, ss)

    def quad(ss, mm):
        return ss * MIDDLE + mm

    q = quad(s, m)
    core_peer = device(h, m, 1 - c, s)
    middle_peer = device(h, 1 - m, c, s)
    shard_peer = device(h, m, c, 1 - s)
    corner_peer = device(h, 1 - m, c, 1 - s)
    quad_peers = [
        (quad(1 - s, 1 - m), corner_peer),
        (quad(s, 1 - m), middle_peer),
        (quad(1 - s, m), shard_peer),
    ]
    high_peers = []
    for e in range(1, high):
        hh = lax.rem(h + e, high)
        high_peers.append((hh, device(hh, m, c, s)))

    barrier = pltpu.get_barrier_semaphore()
    everyone = [core_peer] + [peer for _, peer in high_peers + quad_peers]
    for peer in everyone:
        pl.semaphore_signal(barrier, inc=1, device_id=peer, device_id_type=MESH)

    loading = []

    def load(source, target):
        copy = pltpu.make_async_copy(source, target, loads.at[len(loading)])
        copy.start()
        loading.append(copy)
        return copy

    needed = {}
    for turn, i in enumerate((1 - c, c)):
        needed[turn, "bases"] = load(bases_hbm.at[i], bases.at[i])
        for k, cut in enumerate(cuts):
            needed[turn, k] = load(grads_hbm.at[i, :, cut], grads.at[i, :, cut])
    needed["narrow"] = load(narrow_hbm.at[c], narrow)
    moments = [load(na_one_hbm, na_one), load(na_two_hbm, na_two)]
    for i in range(CORES):
        moments.append(load(sq_one_hbm.at[:, i, :], sq_one.at[i]))
        moments.append(load(sq_two_hbm.at[:, i, :], sq_two.at[i]))

    waited = set()

    def ready(key):
        if key not in waited:
            waited.add(key)
            needed[key].wait()

    def moments_ready():
        while moments:
            moments.pop(0).wait()

    pending = []

    def remote(source, target, peer):
        at = len(pending)
        copy = pltpu.make_async_remote_copy(
            src_ref=source,
            dst_ref=target,
            send_sem=sends.at[at],
            recv_sem=recvs.at[at],
            device_id=peer,
            device_id_type=MESH,
        )
        pending.append(copy)
        return copy

    def send(source, target, peer):
        copy = remote(source, target, peer)
        copy.start()
        return copy

    def wide(value):
        return value.astype(jnp.float32)

    def adam(st, cc, mm, hh=None):
        where = (cc, mm) if hh is None else (cc, mm, hh)
        shape = st.total.shape[len(where) :]
        rows = math.prod(shape[:-1])
        first = mm * rows if hh is None else (mm * high + hh) * rows
        at = pl.ds(pl.multiple_of(first, 8), rows)
        gradient = wide(st.total[where]).reshape(rows, shape[-1])
        direction, one, two = adam_update(
            gradient, st.one[cc, at, st.columns], st.two[cc, at, st.columns]
        )
        st.direction[(cc, s) + where[1:]] = direction.astype(jnp.bfloat16).reshape(shape)
        st.one_out[cc, at, st.columns] = one
        st.two_out[cc, at, st.columns] = two

    def added(value, copies, arrivals):
        total = wide(value)
        for k, copy in enumerate(copies):
            copy.wait_recv()
            total = total + wide(arrivals[k])
        return total.astype(jnp.bfloat16)

    def core_sum(st):
        st.first.wait_recv()
        st.sum1[...] = (wide(st.ours[...]) + wide(st.in1[...])).astype(jnp.bfloat16)

    def quad_first(st):
        core_sum(st)
        second = [
            send(st.sum1.at[qq], st.in2.at[k], peer) for k, (qq, peer) in enumerate(quad_peers)
        ]
        yield
        st.sum2[...] = added(st.sum1[q], second, st.in2)
        third = [
            send(st.sum2.at[hh], st.in3.at[k], peer) for k, (hh, peer) in enumerate(high_peers)
        ]
        yield
        st.total[c, m, h] = added(st.sum2[h], third, st.in3)
        mine = st.total.at[c, m, h]
        back = [send(mine, mine, peer) for _, peer in high_peers]
        yield
        for copy in back:
            copy.wait_recv()
        mine = st.total.at[c, m]
        total_middle = send(mine, mine, middle_peer)
        moments_ready()
        adam(st, c, m)
        mine = st.direction.at[c, s, m]
        shard = send(mine, mine, shard_peer)
        corner = send(mine, mine, corner_peer)
        mine = st.total.at[c, m]
        last = [send(mine, mine, core_peer)]
        yield
        last.pop().wait_recv()
        adam(st, 1 - c, m)
        yield
        shard.wait_recv()
        came = st.direction.at[c, 1 - s, m]
        last.append(send(came, came, core_peer))
        yield
        total_middle.wait_recv()
        came = st.total.at[c, 1 - m]
        total_core = send(came, came, core_peer)
        adam(st, c, 1 - m)
        yield
        corner.wait_recv()
        came = st.direction.at[c, 1 - s, 1 - m]
        last.append(send(came, came, core_peer))
        yield
        total_core.wait_recv()
        adam(st, 1 - c, 1 - m)
        for copy in last:
            copy.wait_recv()

    def high_first(st):
        core_sum(st)
        second = [
            send(st.sum1.at[:, hh], st.in2.at[k], peer) for k, (hh, peer) in enumerate(high_peers)
        ]
        yield
        st.sum2[...] = added(st.sum1[:, h], second, st.in2)
        third = [
            send(st.sum2.at[qq], st.in3.at[k], peer) for k, (qq, peer) in enumerate(quad_peers)
        ]
        yield
        st.total[c, m, h] = added(st.sum2[q], third, st.in3)
        mine = st.total.at[c, m, h]
        back = [send(mine, mine, middle_peer)]
        moments_ready()
        adam(st, c, m, h)
        mine = st.direction.at[c, s, m, h]
        back.append(send(mine, mine, corner_peer))
        back.append(send(mine, mine, shard_peer))
        yield
        for copy in back:
            copy.wait_recv()
        totals, ours = st.total.at[c, :, h], st.direction.at[c, 1 - s, :, h]
        last = []
        for _, peer in high_peers:
            last.append(send(totals, totals, peer))
            last.append(send(ours, ours, peer))
        adam(st, c, 1 - m, h)
        yield
        for copy in last:
            copy.wait_recv()
        totals, ours = st.total.at[c], st.direction.at[c, 1 - s]
        total_core = send(totals, totals, core_peer)
        direction_core = send(ours, ours, core_peer)
        for hh, _ in high_peers:
            for mm in range(MIDDLE):
                adam(st, c, mm, hh)
        yield
        total_core.wait_recv()
        for mm in range(MIDDLE):
            adam(st, 1 - c, mm)
        direction_core.wait_recv()

    def project(turn, i):
        ready((turn, "bases"))
        for k in range(pieces):
            ready((turn, k))
        part = lax.dot_general(
            bases[i], grads[i], (((0,), (0,)), ((), ())), preferred_element_type=jnp.float32
        )
        for k, cut in enumerate(cuts):
            parts[k][i] = part[:, cut].astype(jnp.bfloat16).reshape(parts[k].shape[1:])

    streams = [
        Stream(
            narrow_hbm.at[1 - c],
            narrow,
            buffers[pieces]
            + [directions_out[pieces], na_one, na_two, na_one_out, na_two_out, slice(None)],
        )
    ]
    for k, cut in enumerate(cuts):
        streams.append(
            Stream(
                parts[k].at[1 - c],
                parts[k].at[c],
                buffers[k] + [directions_out[k], sq_one, sq_two, sq_one_out, sq_two_out, cut],
            )
        )
    for st in streams:
        st.first = remote(st.theirs, st.in1, core_peer)
    running = [high_first(streams[0])] + [quad_first(st) for st in streams[1:]]

    pl.semaphore_wait(barrier, len(everyone))
    streams[0].first.start()
    project(0, 1 - c)
    for st in streams[1:]:
        st.first.start()
    ready("narrow")
    next(running[0], None)
    project(1, c)
    for at in sequence(pieces)[1:]:
        next(running[at], None)
    for copy in pending:
        copy.wait_send()


def sequence(pieces):
    square = list(range(1, pieces + 1))
    turns = [0] + square
    turns += square + [0]
    turns += square[:1] + [0] + square[1:]
    turns += square[:1] + [0] + square[1:]
    turns += square
    turns += square[:1] * 3 + [0]
    for k in square[1:]:
        turns += [k] * 3
    return turns + [0] + square


def finish(cuts, bases_ref, *refs):
    sq_dir_refs = refs[: len(cuts)]
    na_dir_ref, sq_one_ref, sq_two_ref, na_one_ref, na_two_ref = refs[len(cuts) : len(cuts) + 5]
    update_out, na_update_out, sq_one_out, sq_two_out, na_one_out, na_two_out = refs[-9:-3]
    update, sems, tile_sems = refs[-3:]
    pairs = [(na_dir_ref, na_update_out), (na_one_ref, na_one_out), (na_two_ref, na_two_out)]
    for i in range(CORES):
        pairs.append((sq_one_ref.at[i], sq_one_out.at[:, i, :]))
        pairs.append((sq_two_ref.at[i], sq_two_out.at[:, i, :]))
    copies = [
        pltpu.make_async_copy(source, target, sems.at[k])
        for k, (source, target) in enumerate(pairs)
    ]
    for copy in copies:
        copy.start()
    height = update.shape[1] // TILES
    for i in range(CORES):
        for t in range(TILES):
            rows = pl.ds(t * height, height)
            for cut, sq_dir_ref in zip(cuts, sq_dir_refs):
                update[i, rows, cut] = jnp.dot(
                    bases_ref[i, rows], sq_dir_ref[i], preferred_element_type=jnp.float32
                ).astype(jnp.bfloat16)
            copy = pltpu.make_async_copy(
                update.at[i, rows], update_out.at[i, rows], tile_sems.at[i, t]
            )
            copy.start()
            copies.append(copy)
    for copy in copies:
        copy.wait()


def kernel_exchange(reps, square, narrow, bases, square_first, square_second, narrow_first, narrow_second):
    matrices, width, columns = square.shape
    rank = bases.shape[2]
    high = reps // (CORES * MIDDLE)
    shards = SHARDS
    quads = shards * MIDDLE
    bf16, f32 = jnp.bfloat16, jnp.float32
    cuts = []
    while sum(cut.stop - cut.start for cut in cuts) < columns:
        begin = cuts[-1].stop if cuts else 0
        size = -(-(columns - begin) // ((PIECES - len(cuts)) * 128)) * 128
        cuts.append(slice(begin, min(columns, begin + size)))
    kinds = [(rank // (quads * high), cut.stop - cut.start) for cut in cuts]
    na = (width // (quads * high), narrow.shape[2])
    kinds.append(na)
    own = (matrices, MIDDLE, high)
    own_square = (matrices, rank // shards, columns)

    buffers = []
    for kind in kinds:
        inner, outer = (quads, high) if kind is na else (high, quads)
        shapes = [
            (quads, high) + kind,
            (quads, high) + kind,
            (outer - 1, inner) + kind,
            (inner,) + kind,
            (inner - 1,) + kind,
            own + kind,
        ]
        buffers += [pltpu.VMEM(shape, bf16) for shape in shapes]
    copies = len(kinds) * (8 + (quads - 1) + 4 * (high - 1))
    vmem = pl.BlockSpec(memory_space=pltpu.VMEM)
    anywhere = pl.BlockSpec(memory_space=pl.ANY)
    out = pl.pallas_call(
        functools.partial(kernel, high, cuts),
        out_shape=tuple(
            [jax.ShapeDtypeStruct((matrices, shards, MIDDLE, high) + kind, bf16) for kind in kinds]
            + [jax.ShapeDtypeStruct(own_square, f32)] * 2
            + [jax.ShapeDtypeStruct(narrow_first.shape, f32)] * 2
        ),
        in_specs=[pl.BlockSpec(memory_space=pltpu.HBM)] * 7,
        out_specs=[vmem] * (len(kinds) + 4),
        scratch_shapes=[
            pltpu.VMEM(square.shape, bf16),
            pltpu.VMEM(bases.shape, bf16),
            pltpu.VMEM((quads, high) + na, bf16),
            pltpu.VMEM(own_square, f32),
            pltpu.VMEM(own_square, f32),
            pltpu.VMEM(narrow_first.shape, f32),
            pltpu.VMEM(narrow_first.shape, f32),
        ]
        + [pltpu.VMEM((matrices, quads, high) + kind, bf16) for kind in kinds[:-1]]
        + buffers
        + [
            pltpu.SemaphoreType.DMA((2 * (1 + len(cuts)) + 3 + 2 * matrices,)),
            pltpu.SemaphoreType.DMA((copies,)),
            pltpu.SemaphoreType.DMA((copies,)),
        ],
        compiler_params=pltpu.CompilerParams(
            collective_id=0, has_side_effects=True, vmem_limit_bytes=48 * 1024 * 1024
        ),
        name="galore_exchange",
    )(
        *[
            pltpu.with_memory_space_constraint(operand, pltpu.HBM)
            for operand in (
                square,
                narrow.reshape((matrices, quads, high) + na),
                bases,
                square_first,
                square_second,
                narrow_first,
                narrow_second,
            )
        ]
    )
    *sq_dirs, na_dir, sq_one, sq_two, na_one, na_two = out
    return pl.pallas_call(
        functools.partial(finish, cuts),
        out_shape=(
            jax.ShapeDtypeStruct(square.shape, bf16),
            jax.ShapeDtypeStruct(narrow.shape, bf16),
            jax.ShapeDtypeStruct(square_first.shape, f32),
            jax.ShapeDtypeStruct(square_second.shape, f32),
            jax.ShapeDtypeStruct(narrow_first.shape, f32),
            jax.ShapeDtypeStruct(narrow_second.shape, f32),
        ),
        in_specs=[vmem] * (6 + len(cuts)),
        out_specs=[anywhere] * 6,
        scratch_shapes=[
            pltpu.VMEM(square.shape, bf16),
            pltpu.SemaphoreType.DMA((7,)),
            pltpu.SemaphoreType.DMA((matrices, TILES)),
        ],
        compiler_params=pltpu.CompilerParams(vmem_limit_bytes=24 * 1024 * 1024),
        name="galore_finish",
    )(
        bases,
        *[part.reshape(matrices, rank, -1) for part in sq_dirs],
        na_dir.reshape(narrow.shape),
        sq_one,
        sq_two,
        na_one,
        na_two,
    )


def on_device(square_grads, narrow_grads, galore_bases, *moments):
    shards, reps = lax.axis_size("shard"), lax.axis_size("rep")
    square, narrow = square_grads[0, 0], narrow_grads[0, 0]
    chunks = shards * reps // CORES
    fits = (
        reps % (CORES * MIDDLE) == 0
        and reps > CORES * MIDDLE
        and shards == SHARDS
        and square.shape[0] == CORES
        and square.shape[2] % 128 == 0
        and square.shape[2] >= PIECES * 128
        and galore_bases.shape[2] % (16 * chunks) == 0
        and square.shape[1] % (8 * chunks) == 0
        and square.shape[1] % (16 * TILES) == 0
    )
    run = functools.partial(kernel_exchange, reps) if fits else plain_exchange
    return run(square, narrow, galore_bases, *moments)


def solution(mesh):
    placed = (
        P("rep", "shard", None, None, None),
        P("rep", "shard", None, None, None),
        P(),
        P("shard", None, None),
        P("shard", None, None),
        P(None, "shard", None),
        P(None, "shard", None),
    )
    return jax.shard_map(
        on_device,
        mesh=mesh,
        in_specs=placed,
        out_specs=(
            P(),
            P(),
            P("shard", None, None),
            P("shard", None, None),
            P(None, "shard", None),
            P(None, "shard", None),
        ),
        check_vma=False,
    )
```

```python
import functools
import math

import jax
import jax.numpy as jnp
from jax import lax
from jax.experimental import pallas as pl
from jax.experimental.pallas import tpu as pltpu
from jax.sharding import PartitionSpec as P

STEP = 1000


beta_one = 0.9
beta_two = 0.999
epsilon = 1e-08
MESH = pl.DeviceIdType.MESH
CORES = 2
MIDDLE = 2
SHARDS = 2
PIECES = 3
TILES = 4


def adam_update(gradient, moment_one, moment_two):
    first_new = beta_one * moment_one + (1.0 - beta_one) * gradient
    second_new = beta_two * moment_two + (1.0 - beta_two) * gradient * gradient
    correct_one = 1.0 - beta_one**STEP
    correct_two = 1.0 - beta_two**STEP
    direction = first_new * (1.0 / correct_one) / (
        jnp.sqrt(second_new * (1.0 / correct_two)) + epsilon
    )
    return (direction, first_new, second_new)


def plain_exchange(square, narrow, bases, square_first, square_second, narrow_first, narrow_second):
    partial = jnp.einsum("imr,imn->rin", bases, square, preferred_element_type=jnp.float32)

    def total(value, axis):
        part = lax.psum_scatter(
            value.astype(jnp.bfloat16), "shard", scatter_dimension=axis, tiled=True
        )
        return lax.psum(part, "rep").astype(jnp.float32)

    square_dir, new_square_first, new_square_second = adam_update(
        total(partial, 0), square_first, square_second
    )
    narrow_dir, new_narrow_first, new_narrow_second = adam_update(
        total(narrow, 1), narrow_first, narrow_second
    )
    directions = lax.all_gather(square_dir.astype(jnp.bfloat16), "shard", axis=0, tiled=True)
    square_update = jnp.einsum(
        "imr,rin->imn", bases, directions, preferred_element_type=jnp.float32
    ).astype(jnp.bfloat16)
    narrow_update = lax.all_gather(narrow_dir.astype(jnp.bfloat16), "shard", axis=1, tiled=True)
    return (
        square_update,
        narrow_update,
        new_square_first,
        new_square_second,
        new_narrow_first,
        new_narrow_second,
    )


class Stream:
    def __init__(self, theirs, ours, refs):
        self.theirs, self.ours = theirs, ours
        (
            self.in1,
            self.sum1,
            self.in2,
            self.sum2,
            self.in3,
            self.total,
            self.direction,
            self.one,
            self.two,
            self.one_out,
            self.two_out,
            self.columns,
        ) = refs


def kernel(high, cuts, *refs):
    pieces = len(cuts)
    refs = list(refs)

    def take(number):
        taken = refs[:number]
        del refs[:number]
        return taken

    grads_hbm, narrow_hbm, bases_hbm, sq_one_hbm, sq_two_hbm, na_one_hbm, na_two_hbm = take(7)
    directions_out = take(pieces + 1)
    sq_one_out, sq_two_out, na_one_out, na_two_out = take(4)
    grads, bases, narrow, sq_one, sq_two, na_one, na_two = take(7)
    parts = take(pieces)
    buffers = [take(6) for _ in range(pieces + 1)]
    loads, sends, recvs = take(3)

    me_rep = lax.axis_index("rep")
    s = lax.axis_index("shard")
    c = lax.rem(me_rep, CORES)
    m = lax.rem(me_rep // CORES, MIDDLE)
    h = me_rep // (CORES * MIDDLE)

    def device(hh, mm, cc, ss):
        return ((hh * MIDDLE + mm) * CORES + cc, ss)

    def quad(ss, mm):
        return ss * MIDDLE + mm

    q = quad(s, m)
    core_peer = device(h, m, 1 - c, s)
    middle_peer = device(h, 1 - m, c, s)
    shard_peer = device(h, m, c, 1 - s)
    corner_peer = device(h, 1 - m, c, 1 - s)
    quad_peers = [
        (quad(1 - s, 1 - m), corner_peer),
        (quad(s, 1 - m), middle_peer),
        (quad(1 - s, m), shard_peer),
    ]
    high_peers = []
    for e in range(1, high):
        hh = lax.rem(h + e, high)
        high_peers.append((hh, device(hh, m, c, s)))

    barrier = pltpu.get_barrier_semaphore()
    everyone = [core_peer] + [peer for _, peer in high_peers + quad_peers]
    for peer in everyone:
        pl.semaphore_signal(barrier, inc=1, device_id=peer, device_id_type=MESH)

    loading = []

    def load(source, target):
        copy = pltpu.make_async_copy(source, target, loads.at[len(loading)])
        copy.start()
        loading.append(copy)
        return copy

    needed = {}

    def load_matrix(turn, i):
        needed[turn, "bases"] = load(bases_hbm.at[i], bases.at[i])
        for k, cut in enumerate(cuts):
            needed[turn, k] = load(grads_hbm.at[i, :, cut], grads.at[i, :, cut])

    load_matrix(0, 1 - c)
    needed["narrow"] = load(narrow_hbm.at[c], narrow)
    moments = []

    def load_moments():
        moments.extend((load(na_one_hbm, na_one), load(na_two_hbm, na_two)))
        for i in range(CORES):
            moments.append(load(sq_one_hbm.at[:, i, :], sq_one.at[i]))
            moments.append(load(sq_two_hbm.at[:, i, :], sq_two.at[i]))

    waited = set()

    def ready(key):
        if key not in waited:
            waited.add(key)
            needed[key].wait()

    def moments_ready():
        while moments:
            moments.pop(0).wait()

    pending = []

    def remote(source, target, peer):
        at = len(pending)
        copy = pltpu.make_async_remote_copy(
            src_ref=source,
            dst_ref=target,
            send_sem=sends.at[at],
            recv_sem=recvs.at[at],
            device_id=peer,
            device_id_type=MESH,
        )
        pending.append(copy)
        return copy

    def send(source, target, peer):
        copy = remote(source, target, peer)
        copy.start()
        return copy

    def wide(value):
        return value.astype(jnp.float32)

    def adam(st, cc, mm, hh=None):
        where = (cc, mm) if hh is None else (cc, mm, hh)
        shape = st.total.shape[len(where) :]
        rows = math.prod(shape[:-1])
        first = mm * rows if hh is None else (mm * high + hh) * rows
        at = pl.ds(pl.multiple_of(first, 8), rows)
        gradient = wide(st.total[where]).reshape(rows, shape[-1])
        direction, one, two = adam_update(
            gradient, st.one[cc, at, st.columns], st.two[cc, at, st.columns]
        )
        st.direction[(cc, s) + where[1:]] = direction.astype(jnp.bfloat16).reshape(shape)
        st.one_out[cc, at, st.columns] = one
        st.two_out[cc, at, st.columns] = two

    def added(value, copies, arrivals):
        total = wide(value)
        for k, copy in enumerate(copies):
            copy.wait_recv()
            total = total + wide(arrivals[k])
        return total.astype(jnp.bfloat16)

    def core_sum(st):
        st.first.wait_recv()
        st.sum1[...] = (wide(st.ours[...]) + wide(st.in1[...])).astype(jnp.bfloat16)

    def quad_first(st):
        core_sum(st)
        second = [
            send(st.sum1.at[qq], st.in2.at[k], peer) for k, (qq, peer) in enumerate(quad_peers)
        ]
        yield
        st.sum2[...] = added(st.sum1[q], second, st.in2)
        third = [
            send(st.sum2.at[hh], st.in3.at[k], peer) for k, (hh, peer) in enumerate(high_peers)
        ]
        yield
        st.total[c, m, h] = added(st.sum2[h], third, st.in3)
        mine = st.total.at[c, m, h]
        back = [send(mine, mine, peer) for _, peer in high_peers]
        yield
        for copy in back:
            copy.wait_recv()
        mine = st.total.at[c, m]
        total_middle = send(mine, mine, middle_peer)
        moments_ready()
        adam(st, c, m)
        mine = st.direction.at[c, s, m]
        shard = send(mine, mine, shard_peer)
        corner = send(mine, mine, corner_peer)
        mine = st.total.at[c, m]
        last = [send(mine, mine, core_peer)]
        yield
        last.pop().wait_recv()
        adam(st, 1 - c, m)
        yield
        shard.wait_recv()
        came = st.direction.at[c, 1 - s, m]
        last.append(send(came, came, core_peer))
        yield
        total_middle.wait_recv()
        came = st.total.at[c, 1 - m]
        total_core = send(came, came, core_peer)
        adam(st, c, 1 - m)
        yield
        corner.wait_recv()
        came = st.direction.at[c, 1 - s, 1 - m]
        last.append(send(came, came, core_peer))
        yield
        total_core.wait_recv()
        adam(st, 1 - c, 1 - m)
        for copy in last:
            copy.wait_recv()

    def high_first(st):
        core_sum(st)
        second = [
            send(st.sum1.at[:, hh], st.in2.at[k], peer) for k, (hh, peer) in enumerate(high_peers)
        ]
        yield
        st.sum2[...] = added(st.sum1[:, h], second, st.in2)
        third = [
            send(st.sum2.at[qq], st.in3.at[k], peer) for k, (qq, peer) in enumerate(quad_peers)
        ]
        yield
        st.total[c, m, h] = added(st.sum2[q], third, st.in3)
        mine = st.total.at[c, m, h]
        back = [send(mine, mine, middle_peer)]
        moments_ready()
        adam(st, c, m, h)
        mine = st.direction.at[c, s, m, h]
        back.append(send(mine, mine, corner_peer))
        back.append(send(mine, mine, shard_peer))
        yield
        for copy in back:
            copy.wait_recv()
        totals, ours = st.total.at[c, :, h], st.direction.at[c, 1 - s, :, h]
        last = []
        for _, peer in high_peers:
            last.append(send(totals, totals, peer))
            last.append(send(ours, ours, peer))
        adam(st, c, 1 - m, h)
        yield
        for copy in last:
            copy.wait_recv()
        totals, ours = st.total.at[c], st.direction.at[c, 1 - s]
        total_core = send(totals, totals, core_peer)
        direction_core = send(ours, ours, core_peer)
        for hh, _ in high_peers:
            for mm in range(MIDDLE):
                adam(st, c, mm, hh)
        yield
        total_core.wait_recv()
        for mm in range(MIDDLE):
            adam(st, 1 - c, mm)
        direction_core.wait_recv()

    def matrix_ready(turn):
        ready((turn, "bases"))
        for k in range(pieces):
            ready((turn, k))

    def project(turn, i):
        matrix_ready(turn)
        part = lax.dot_general(
            bases[i], grads[i], (((0,), (0,)), ((), ())), preferred_element_type=jnp.float32
        )
        for k, cut in enumerate(cuts):
            parts[k][i] = part[:, cut].astype(jnp.bfloat16).reshape(parts[k].shape[1:])

    streams = [
        Stream(
            narrow_hbm.at[1 - c],
            narrow,
            buffers[pieces]
            + [directions_out[pieces], na_one, na_two, na_one_out, na_two_out, slice(None)],
        )
    ]
    for k, cut in enumerate(cuts):
        streams.append(
            Stream(
                parts[k].at[1 - c],
                parts[k].at[c],
                buffers[k] + [directions_out[k], sq_one, sq_two, sq_one_out, sq_two_out, cut],
            )
        )
    for st in streams:
        st.first = remote(st.theirs, st.in1, core_peer)
    running = [high_first(streams[0])] + [quad_first(st) for st in streams[1:]]

    load_matrix(1, c)
    pl.semaphore_wait(barrier, len(everyone))
    streams[0].first.start()
    project(0, 1 - c)
    for st in streams[1:]:
        st.first.start()
    ready("narrow")
    next(running[0], None)
    project(1, c)
    load_moments()
    for at in sequence(pieces)[1:]:
        next(running[at], None)
    for copy in pending:
        copy.wait_send()


def sequence(pieces):
    square = list(range(1, pieces + 1))
    turns = [0] + square
    turns += square + [0]
    turns += square[:1] + [0] + square[1:]
    turns += square[:1] + [0] + square[1:]
    turns += square
    turns += square[:1] * 3 + [0]
    for k in square[1:]:
        turns += [k] * 3
    return turns + [0] + square


def finish(cuts, bases_ref, *refs):
    sq_dir_refs = refs[: len(cuts)]
    na_dir_ref, sq_one_ref, sq_two_ref, na_one_ref, na_two_ref = refs[len(cuts) : len(cuts) + 5]
    update_out, na_update_out, sq_one_out, sq_two_out, na_one_out, na_two_out = refs[-9:-3]
    update, sems, tile_sems = refs[-3:]
    pairs = [(na_dir_ref, na_update_out), (na_one_ref, na_one_out), (na_two_ref, na_two_out)]
    for i in range(CORES):
        pairs.append((sq_one_ref.at[i], sq_one_out.at[:, i, :]))
        pairs.append((sq_two_ref.at[i], sq_two_out.at[:, i, :]))
    copies = [
        pltpu.make_async_copy(source, target, sems.at[k])
        for k, (source, target) in enumerate(pairs)
    ]
    for copy in copies:
        copy.start()
    height = update.shape[1] // TILES
    for i in range(CORES):
        for t in range(TILES):
            rows = pl.ds(t * height, height)
            for cut, sq_dir_ref in zip(cuts, sq_dir_refs):
                update[i, rows, cut] = jnp.dot(
                    bases_ref[i, rows], sq_dir_ref[i], preferred_element_type=jnp.float32
                ).astype(jnp.bfloat16)
            copy = pltpu.make_async_copy(
                update.at[i, rows], update_out.at[i, rows], tile_sems.at[i, t]
            )
            copy.start()
            copies.append(copy)
    for copy in copies:
        copy.wait()


def kernel_exchange(reps, square, narrow, bases, square_first, square_second, narrow_first, narrow_second):
    matrices, width, columns = square.shape
    rank = bases.shape[2]
    high = reps // (CORES * MIDDLE)
    shards = SHARDS
    quads = shards * MIDDLE
    bf16, f32 = jnp.bfloat16, jnp.float32
    cuts = []
    while sum(cut.stop - cut.start for cut in cuts) < columns:
        begin = cuts[-1].stop if cuts else 0
        size = -(-(columns - begin) // ((PIECES - len(cuts)) * 128)) * 128
        cuts.append(slice(begin, min(columns, begin + size)))
    kinds = [(rank // (quads * high), cut.stop - cut.start) for cut in cuts]
    na = (width // (quads * high), narrow.shape[2])
    kinds.append(na)
    own = (matrices, MIDDLE, high)
    own_square = (matrices, rank // shards, columns)

    buffers = []
    for kind in kinds:
        inner, outer = (quads, high) if kind is na else (high, quads)
        shapes = [
            (quads, high) + kind,
            (quads, high) + kind,
            (outer - 1, inner) + kind,
            (inner,) + kind,
            (inner - 1,) + kind,
            own + kind,
        ]
        buffers += [pltpu.VMEM(shape, bf16) for shape in shapes]
    copies = len(kinds) * (8 + (quads - 1) + 4 * (high - 1))
    vmem = pl.BlockSpec(memory_space=pltpu.VMEM)
    anywhere = pl.BlockSpec(memory_space=pl.ANY)
    out = pl.pallas_call(
        functools.partial(kernel, high, cuts),
        out_shape=tuple(
            [jax.ShapeDtypeStruct((matrices, shards, MIDDLE, high) + kind, bf16) for kind in kinds]
            + [jax.ShapeDtypeStruct(own_square, f32)] * 2
            + [jax.ShapeDtypeStruct(narrow_first.shape, f32)] * 2
        ),
        in_specs=[pl.BlockSpec(memory_space=pltpu.HBM)] * 7,
        out_specs=[vmem] * (len(kinds) + 4),
        scratch_shapes=[
            pltpu.VMEM(square.shape, bf16),
            pltpu.VMEM(bases.shape, bf16),
            pltpu.VMEM((quads, high) + na, bf16),
            pltpu.VMEM(own_square, f32),
            pltpu.VMEM(own_square, f32),
            pltpu.VMEM(narrow_first.shape, f32),
            pltpu.VMEM(narrow_first.shape, f32),
        ]
        + [pltpu.VMEM((matrices, quads, high) + kind, bf16) for kind in kinds[:-1]]
        + buffers
        + [
            pltpu.SemaphoreType.DMA((2 * (1 + len(cuts)) + 3 + 2 * matrices,)),
            pltpu.SemaphoreType.DMA((copies,)),
            pltpu.SemaphoreType.DMA((copies,)),
        ],
        compiler_params=pltpu.CompilerParams(
            collective_id=0, has_side_effects=True, vmem_limit_bytes=48 * 1024 * 1024
        ),
        name="galore_exchange",
    )(
        *[
            pltpu.with_memory_space_constraint(operand, pltpu.HBM)
            for operand in (
                square,
                narrow.reshape((matrices, quads, high) + na),
                bases,
                square_first,
                square_second,
                narrow_first,
                narrow_second,
            )
        ]
    )
    *sq_dirs, na_dir, sq_one, sq_two, na_one, na_two = out
    return pl.pallas_call(
        functools.partial(finish, cuts),
        out_shape=(
            jax.ShapeDtypeStruct(square.shape, bf16),
            jax.ShapeDtypeStruct(narrow.shape, bf16),
            jax.ShapeDtypeStruct(square_first.shape, f32),
            jax.ShapeDtypeStruct(square_second.shape, f32),
            jax.ShapeDtypeStruct(narrow_first.shape, f32),
            jax.ShapeDtypeStruct(narrow_second.shape, f32),
        ),
        in_specs=[vmem] * (6 + len(cuts)),
        out_specs=[anywhere] * 6,
        scratch_shapes=[
            pltpu.VMEM(square.shape, bf16),
            pltpu.SemaphoreType.DMA((7,)),
            pltpu.SemaphoreType.DMA((matrices, TILES)),
        ],
        compiler_params=pltpu.CompilerParams(vmem_limit_bytes=24 * 1024 * 1024),
        name="galore_finish",
    )(
        bases,
        *[part.reshape(matrices, rank, -1) for part in sq_dirs],
        na_dir.reshape(narrow.shape),
        sq_one,
        sq_two,
        na_one,
        na_two,
    )


def on_device(square_grads, narrow_grads, galore_bases, *moments):
    shards, reps = lax.axis_size("shard"), lax.axis_size("rep")
    square, narrow = square_grads[0, 0], narrow_grads[0, 0]
    chunks = shards * reps // CORES
    fits = (
        reps % (CORES * MIDDLE) == 0
        and reps > CORES * MIDDLE
        and shards == SHARDS
        and square.shape[0] == CORES
        and square.shape[2] % 128 == 0
        and square.shape[2] >= PIECES * 128
        and galore_bases.shape[2] % (16 * chunks) == 0
        and square.shape[1] % (8 * chunks) == 0
        and square.shape[1] % (16 * TILES) == 0
    )
    run = functools.partial(kernel_exchange, reps) if fits else plain_exchange
    return run(square, narrow, galore_bases, *moments)


def solution(mesh):
    placed = (
        P("rep", "shard", None, None, None),
        P("rep", "shard", None, None, None),
        P(),
        P("shard", None, None),
        P("shard", None, None),
        P(None, "shard", None),
        P(None, "shard", None),
    )
    return jax.shard_map(
        on_device,
        mesh=mesh,
        in_specs=placed,
        out_specs=(
            P(),
            P(),
            P("shard", None, None),
            P("shard", None, None),
            P(None, "shard", None),
            P(None, "shard", None),
        ),
        check_vma=False,
    )
```

```python
import functools
import math

import jax
import jax.numpy as jnp
from jax import lax
from jax.experimental import pallas as pl
from jax.experimental.pallas import tpu as pltpu
from jax.sharding import PartitionSpec as P

STEP = 1000


beta_one = 0.9
beta_two = 0.999
epsilon = 1e-08
MESH = pl.DeviceIdType.MESH
CORES = 2
MIDDLE = 2
SHARDS = 2
PIECES = 3
LAG = 10
TILES = 4


def adam_update(gradient, moment_one, moment_two):
    first_new = beta_one * moment_one + (1.0 - beta_one) * gradient
    second_new = beta_two * moment_two + (1.0 - beta_two) * gradient * gradient
    correct_one = 1.0 - beta_one**STEP
    correct_two = 1.0 - beta_two**STEP
    direction = first_new * (1.0 / correct_one) / (
        jnp.sqrt(second_new * (1.0 / correct_two)) + epsilon
    )
    return (direction, first_new, second_new)


def plain_exchange(square, narrow, bases, square_first, square_second, narrow_first, narrow_second):
    partial = jnp.einsum("imr,imn->rin", bases, square, preferred_element_type=jnp.float32)

    def total(value, axis):
        part = lax.psum_scatter(
            value.astype(jnp.bfloat16), "shard", scatter_dimension=axis, tiled=True
        )
        return lax.psum(part, "rep").astype(jnp.float32)

    square_dir, new_square_first, new_square_second = adam_update(
        total(partial, 0), square_first, square_second
    )
    narrow_dir, new_narrow_first, new_narrow_second = adam_update(
        total(narrow, 1), narrow_first, narrow_second
    )
    directions = lax.all_gather(square_dir.astype(jnp.bfloat16), "shard", axis=0, tiled=True)
    square_update = jnp.einsum(
        "imr,rin->imn", bases, directions, preferred_element_type=jnp.float32
    ).astype(jnp.bfloat16)
    narrow_update = lax.all_gather(narrow_dir.astype(jnp.bfloat16), "shard", axis=1, tiled=True)
    return (
        square_update,
        narrow_update,
        new_square_first,
        new_square_second,
        new_narrow_first,
        new_narrow_second,
    )


class Stream:
    def __init__(self, theirs, ours, refs):
        self.theirs, self.ours = theirs, ours
        (
            self.in1,
            self.sum1,
            self.in2,
            self.sum2,
            self.in3,
            self.total,
            self.direction,
            self.one,
            self.two,
            self.one_out,
            self.two_out,
            self.columns,
        ) = refs


def kernel(high, cuts, *refs):
    pieces = len(cuts)
    refs = list(refs)

    def take(number):
        taken = refs[:number]
        del refs[:number]
        return taken

    grads_hbm, narrow_hbm, bases_hbm, sq_one_hbm, sq_two_hbm, na_one_hbm, na_two_hbm = take(7)
    directions_out = take(pieces + 1)
    sq_one_out, sq_two_out, na_one_out, na_two_out = take(4)
    grads, bases, narrow, sq_one, sq_two, na_one, na_two = take(7)
    parts = take(pieces)
    buffers = [take(6) for _ in range(pieces + 1)]
    loads, sends, recvs = take(3)

    me_rep = lax.axis_index("rep")
    s = lax.axis_index("shard")
    c = lax.rem(me_rep, CORES)
    m = lax.rem(me_rep // CORES, MIDDLE)
    h = me_rep // (CORES * MIDDLE)

    def device(hh, mm, cc, ss):
        return ((hh * MIDDLE + mm) * CORES + cc, ss)

    def quad(ss, mm):
        return ss * MIDDLE + mm

    q = quad(s, m)
    core_peer = device(h, m, 1 - c, s)
    middle_peer = device(h, 1 - m, c, s)
    shard_peer = device(h, m, c, 1 - s)
    corner_peer = device(h, 1 - m, c, 1 - s)
    quad_peers = [
        (quad(1 - s, 1 - m), corner_peer),
        (quad(s, 1 - m), middle_peer),
        (quad(1 - s, m), shard_peer),
    ]
    high_peers = []
    for e in range(1, high):
        hh = lax.rem(h + e, high)
        high_peers.append((hh, device(hh, m, c, s)))

    barrier = pltpu.get_barrier_semaphore()
    everyone = [core_peer] + [peer for _, peer in high_peers + quad_peers]
    for peer in everyone:
        pl.semaphore_signal(barrier, inc=1, device_id=peer, device_id_type=MESH)

    loading = []

    def load(source, target):
        copy = pltpu.make_async_copy(source, target, loads.at[len(loading)])
        copy.start()
        loading.append(copy)
        return copy

    needed = {}

    def load_matrix(turn, i):
        needed[turn, "bases"] = load(bases_hbm.at[i], bases.at[i])
        for k, cut in enumerate(cuts):
            needed[turn, k] = load(grads_hbm.at[i, :, cut], grads.at[i, :, cut])

    load_matrix(0, 1 - c)
    needed["narrow"] = load(narrow_hbm.at[c], narrow)
    moments = []

    def load_moments():
        moments.extend((load(na_one_hbm, na_one), load(na_two_hbm, na_two)))
        for i in range(CORES):
            moments.append(load(sq_one_hbm.at[:, i, :], sq_one.at[i]))
            moments.append(load(sq_two_hbm.at[:, i, :], sq_two.at[i]))

    waited = set()

    def ready(key):
        if key not in waited:
            waited.add(key)
            needed[key].wait()

    def moments_ready():
        while moments:
            moments.pop(0).wait()

    pending = []

    def remote(source, target, peer):
        at = len(pending)
        copy = pltpu.make_async_remote_copy(
            src_ref=source,
            dst_ref=target,
            send_sem=sends.at[at],
            recv_sem=recvs.at[at],
            device_id=peer,
            device_id_type=MESH,
        )
        pending.append(copy)
        return copy

    def send(source, target, peer):
        copy = remote(source, target, peer)
        copy.start()
        return copy

    def wide(value):
        return value.astype(jnp.float32)

    def adam(st, cc, mm, hh=None):
        where = (cc, mm) if hh is None else (cc, mm, hh)
        shape = st.total.shape[len(where) :]
        rows = math.prod(shape[:-1])
        first = mm * rows if hh is None else (mm * high + hh) * rows
        at = pl.ds(pl.multiple_of(first, 8), rows)
        gradient = wide(st.total[where]).reshape(rows, shape[-1])
        direction, one, two = adam_update(
            gradient, st.one[cc, at, st.columns], st.two[cc, at, st.columns]
        )
        st.direction[(cc, s) + where[1:]] = direction.astype(jnp.bfloat16).reshape(shape)
        st.one_out[cc, at, st.columns] = one
        st.two_out[cc, at, st.columns] = two

    def added(value, copies, arrivals):
        total = wide(value)
        for k, copy in enumerate(copies):
            copy.wait_recv()
            total = total + wide(arrivals[k])
        return total.astype(jnp.bfloat16)

    def core_sum(st, at):
        st.sum1[at] = (wide(st.ours[at]) + wide(st.in1[at])).astype(jnp.bfloat16)

    def quad_first(st):
        st.first.wait_recv()
        second = []
        for k, (qq, peer) in enumerate(quad_peers):
            core_sum(st, qq)
            second.append(send(st.sum1.at[qq], st.in2.at[k], peer))
        core_sum(st, q)
        yield
        st.sum2[...] = added(st.sum1[q], second, st.in2)
        third = [
            send(st.sum2.at[hh], st.in3.at[k], peer) for k, (hh, peer) in enumerate(high_peers)
        ]
        yield
        st.total[c, m, h] = added(st.sum2[h], third, st.in3)
        mine = st.total.at[c, m, h]
        back = [send(mine, mine, peer) for _, peer in high_peers]
        yield
        for copy in back:
            copy.wait_recv()
        mine = st.total.at[c, m]
        total_middle = send(mine, mine, middle_peer)
        moments_ready()
        adam(st, c, m)
        mine = st.direction.at[c, s, m]
        shard = send(mine, mine, shard_peer)
        corner = send(mine, mine, corner_peer)
        mine = st.total.at[c, m]
        last = [send(mine, mine, core_peer)]
        yield
        last.pop().wait_recv()
        adam(st, 1 - c, m)
        yield
        shard.wait_recv()
        came = st.direction.at[c, 1 - s, m]
        last.append(send(came, came, core_peer))
        yield
        total_middle.wait_recv()
        came = st.total.at[c, 1 - m]
        total_core = send(came, came, core_peer)
        adam(st, c, 1 - m)
        yield
        corner.wait_recv()
        came = st.direction.at[c, 1 - s, 1 - m]
        last.append(send(came, came, core_peer))
        yield
        total_core.wait_recv()
        adam(st, 1 - c, 1 - m)
        for copy in last:
            copy.wait_recv()

    def high_first(st):
        st.first.wait_recv()
        second = []
        for k, (hh, peer) in enumerate(high_peers):
            core_sum(st, (slice(None), hh))
            second.append(send(st.sum1.at[:, hh], st.in2.at[k], peer))
        core_sum(st, (slice(None), h))
        yield
        st.sum2[...] = added(st.sum1[:, h], second, st.in2)
        third = [
            send(st.sum2.at[qq], st.in3.at[k], peer) for k, (qq, peer) in enumerate(quad_peers)
        ]
        yield
        st.total[c, m, h] = added(st.sum2[q], third, st.in3)
        mine = st.total.at[c, m, h]
        back = [send(mine, mine, middle_peer)]
        moments_ready()
        adam(st, c, m, h)
        mine = st.direction.at[c, s, m, h]
        back.append(send(mine, mine, corner_peer))
        back.append(send(mine, mine, shard_peer))
        yield
        for copy in back:
            copy.wait_recv()
        totals, ours = st.total.at[c, :, h], st.direction.at[c, 1 - s, :, h]
        last = []
        for _, peer in high_peers:
            last.append(send(totals, totals, peer))
            last.append(send(ours, ours, peer))
        adam(st, c, 1 - m, h)
        yield
        for copy in last:
            copy.wait_recv()
        totals, ours = st.total.at[c], st.direction.at[c, 1 - s]
        total_core = send(totals, totals, core_peer)
        direction_core = send(ours, ours, core_peer)
        for hh, _ in high_peers:
            for mm in range(MIDDLE):
                adam(st, c, mm, hh)
        yield
        total_core.wait_recv()
        for mm in range(MIDDLE):
            adam(st, 1 - c, mm)
        direction_core.wait_recv()

    def matrix_ready(turn):
        ready((turn, "bases"))
        for k in range(pieces):
            ready((turn, k))

    def project(turn, i):
        matrix_ready(turn)
        part = lax.dot_general(
            bases[i], grads[i], (((0,), (0,)), ((), ())), preferred_element_type=jnp.float32
        )
        for k, cut in enumerate(cuts):
            parts[k][i] = part[:, cut].astype(jnp.bfloat16).reshape(parts[k].shape[1:])

    streams = [
        Stream(
            narrow_hbm.at[1 - c],
            narrow,
            buffers[pieces]
            + [directions_out[pieces], na_one, na_two, na_one_out, na_two_out, slice(None)],
        )
    ]
    for k, cut in enumerate(cuts):
        streams.append(
            Stream(
                parts[k].at[1 - c],
                parts[k].at[c],
                buffers[k] + [directions_out[k], sq_one, sq_two, sq_one_out, sq_two_out, cut],
            )
        )
    for st in streams:
        st.first = remote(st.theirs, st.in1, core_peer)
    running = [high_first(streams[0])] + [quad_first(st) for st in streams[1:]]

    load_matrix(1, c)
    pl.semaphore_wait(barrier, len(everyone))
    streams[0].first.start()
    project(0, 1 - c)
    for st in streams[1:]:
        st.first.start()
    ready("narrow")
    next(running[0], None)
    project(1, c)
    load_moments()
    sent, marks = 0, []
    for turn, at in enumerate(sequence(pieces)[1:]):
        while turn >= LAG and sent < marks[turn - LAG]:
            pending[sent].wait_send()
            sent += 1
        next(running[at], None)
        marks.append(len(pending))
    for copy in pending[sent:]:
        copy.wait_send()


def sequence(pieces):
    square = list(range(1, pieces + 1))
    turns = [0] + square
    turns += square + [0]
    turns += square[:1] + [0] + square[1:]
    turns += square[:1] + [0] + square[1:]
    turns += square
    turns += square[:1] * 3 + [0]
    for k in square[1:]:
        turns += [k] * 3
    return turns + [0] + square


def finish(cuts, bases_ref, *refs):
    sq_dir_refs = refs[: len(cuts)]
    na_dir_ref, sq_one_ref, sq_two_ref, na_one_ref, na_two_ref = refs[len(cuts) : len(cuts) + 5]
    update_out, na_update_out, sq_one_out, sq_two_out, na_one_out, na_two_out = refs[-9:-3]
    update, sems, tile_sems = refs[-3:]
    pairs = [(na_dir_ref, na_update_out), (na_one_ref, na_one_out), (na_two_ref, na_two_out)]
    for i in range(CORES):
        pairs.append((sq_one_ref.at[i], sq_one_out.at[:, i, :]))
        pairs.append((sq_two_ref.at[i], sq_two_out.at[:, i, :]))
    copies = [
        pltpu.make_async_copy(source, target, sems.at[k])
        for k, (source, target) in enumerate(pairs)
    ]
    for copy in copies:
        copy.start()
    height = update.shape[1] // TILES
    for i in range(CORES):
        for t in range(TILES):
            rows = pl.ds(t * height, height)
            for cut, sq_dir_ref in zip(cuts, sq_dir_refs):
                update[i, rows, cut] = jnp.dot(
                    bases_ref[i, rows], sq_dir_ref[i], preferred_element_type=jnp.float32
                ).astype(jnp.bfloat16)
            copy = pltpu.make_async_copy(
                update.at[i, rows], update_out.at[i, rows], tile_sems.at[i, t]
            )
            copy.start()
            copies.append(copy)
    for copy in copies:
        copy.wait()


def kernel_exchange(reps, square, narrow, bases, square_first, square_second, narrow_first, narrow_second):
    matrices, width, columns = square.shape
    rank = bases.shape[2]
    high = reps // (CORES * MIDDLE)
    shards = SHARDS
    quads = shards * MIDDLE
    bf16, f32 = jnp.bfloat16, jnp.float32
    cuts = []
    while sum(cut.stop - cut.start for cut in cuts) < columns:
        begin = cuts[-1].stop if cuts else 0
        size = -(-(columns - begin) // ((PIECES - len(cuts)) * 128)) * 128
        cuts.append(slice(begin, min(columns, begin + size)))
    kinds = [(rank // (quads * high), cut.stop - cut.start) for cut in cuts]
    na = (width // (quads * high), narrow.shape[2])
    kinds.append(na)
    own = (matrices, MIDDLE, high)
    own_square = (matrices, rank // shards, columns)

    buffers = []
    for kind in kinds:
        inner, outer = (quads, high) if kind is na else (high, quads)
        shapes = [
            (quads, high) + kind,
            (quads, high) + kind,
            (outer - 1, inner) + kind,
            (inner,) + kind,
            (inner - 1,) + kind,
            own + kind,
        ]
        buffers += [pltpu.VMEM(shape, bf16) for shape in shapes]
    copies = len(kinds) * (8 + (quads - 1) + 4 * (high - 1))
    vmem = pl.BlockSpec(memory_space=pltpu.VMEM)
    anywhere = pl.BlockSpec(memory_space=pl.ANY)
    out = pl.pallas_call(
        functools.partial(kernel, high, cuts),
        out_shape=tuple(
            [jax.ShapeDtypeStruct((matrices, shards, MIDDLE, high) + kind, bf16) for kind in kinds]
            + [jax.ShapeDtypeStruct(own_square, f32)] * 2
            + [jax.ShapeDtypeStruct(narrow_first.shape, f32)] * 2
        ),
        in_specs=[pl.BlockSpec(memory_space=pltpu.HBM)] * 7,
        out_specs=[vmem] * (len(kinds) + 4),
        scratch_shapes=[
            pltpu.VMEM(square.shape, bf16),
            pltpu.VMEM(bases.shape, bf16),
            pltpu.VMEM((quads, high) + na, bf16),
            pltpu.VMEM(own_square, f32),
            pltpu.VMEM(own_square, f32),
            pltpu.VMEM(narrow_first.shape, f32),
            pltpu.VMEM(narrow_first.shape, f32),
        ]
        + [pltpu.VMEM((matrices, quads, high) + kind, bf16) for kind in kinds[:-1]]
        + buffers
        + [
            pltpu.SemaphoreType.DMA((2 * (1 + len(cuts)) + 3 + 2 * matrices,)),
            pltpu.SemaphoreType.DMA((copies,)),
            pltpu.SemaphoreType.DMA((copies,)),
        ],
        compiler_params=pltpu.CompilerParams(
            collective_id=0, has_side_effects=True, vmem_limit_bytes=48 * 1024 * 1024
        ),
        name="galore_exchange",
    )(
        *[
            pltpu.with_memory_space_constraint(operand, pltpu.HBM)
            for operand in (
                square,
                narrow.reshape((matrices, quads, high) + na),
                bases,
                square_first,
                square_second,
                narrow_first,
                narrow_second,
            )
        ]
    )
    *sq_dirs, na_dir, sq_one, sq_two, na_one, na_two = out
    return pl.pallas_call(
        functools.partial(finish, cuts),
        out_shape=(
            jax.ShapeDtypeStruct(square.shape, bf16),
            jax.ShapeDtypeStruct(narrow.shape, bf16),
            jax.ShapeDtypeStruct(square_first.shape, f32),
            jax.ShapeDtypeStruct(square_second.shape, f32),
            jax.ShapeDtypeStruct(narrow_first.shape, f32),
            jax.ShapeDtypeStruct(narrow_second.shape, f32),
        ),
        in_specs=[vmem] * (6 + len(cuts)),
        out_specs=[anywhere] * 6,
        scratch_shapes=[
            pltpu.VMEM(square.shape, bf16),
            pltpu.SemaphoreType.DMA((7,)),
            pltpu.SemaphoreType.DMA((matrices, TILES)),
        ],
        compiler_params=pltpu.CompilerParams(vmem_limit_bytes=24 * 1024 * 1024),
        name="galore_finish",
    )(
        bases,
        *[part.reshape(matrices, rank, -1) for part in sq_dirs],
        na_dir.reshape(narrow.shape),
        sq_one,
        sq_two,
        na_one,
        na_two,
    )


def on_device(square_grads, narrow_grads, galore_bases, *moments):
    shards, reps = lax.axis_size("shard"), lax.axis_size("rep")
    square, narrow = square_grads[0, 0], narrow_grads[0, 0]
    chunks = shards * reps // CORES
    fits = (
        reps % (CORES * MIDDLE) == 0
        and reps > CORES * MIDDLE
        and shards == SHARDS
        and square.shape[0] == CORES
        and square.shape[2] % 128 == 0
        and square.shape[2] >= PIECES * 128
        and galore_bases.shape[2] % (16 * chunks) == 0
        and square.shape[1] % (8 * chunks) == 0
        and square.shape[1] % (16 * TILES) == 0
    )
    run = functools.partial(kernel_exchange, reps) if fits else plain_exchange
    return run(square, narrow, galore_bases, *moments)


def solution(mesh):
    placed = (
        P("rep", "shard", None, None, None),
        P("rep", "shard", None, None, None),
        P(),
        P("shard", None, None),
        P("shard", None, None),
        P(None, "shard", None),
        P(None, "shard", None),
    )
    return jax.shard_map(
        on_device,
        mesh=mesh,
        in_specs=placed,
        out_specs=(
            P(),
            P(),
            P("shard", None, None),
            P("shard", None, None),
            P(None, "shard", None),
            P(None, "shard", None),
        ),
        check_vma=False,
    )
```

```python
import functools
import math

import jax
import jax.numpy as jnp
from jax import lax
from jax.experimental import pallas as pl
from jax.experimental.pallas import tpu as pltpu
from jax.sharding import PartitionSpec as P

STEP = 1000


beta_one = 0.9
beta_two = 0.999
epsilon = 1e-08
MESH = pl.DeviceIdType.MESH
CORES = 2
MIDDLE = 2
SHARDS = 2
PIECES = 3
HALVES = 1
TILES = 4


def adam_update(gradient, moment_one, moment_two):
    first_new = beta_one * moment_one + (1.0 - beta_one) * gradient
    second_new = beta_two * moment_two + (1.0 - beta_two) * gradient * gradient
    correct_one = 1.0 - beta_one**STEP
    correct_two = 1.0 - beta_two**STEP
    direction = first_new * (1.0 / correct_one) / (
        jnp.sqrt(second_new * (1.0 / correct_two)) + epsilon
    )
    return (direction, first_new, second_new)


def plain_exchange(square, narrow, bases, square_first, square_second, narrow_first, narrow_second):
    partial = jnp.einsum("imr,imn->rin", bases, square, preferred_element_type=jnp.float32)

    def total(value, axis):
        part = lax.psum_scatter(
            value.astype(jnp.bfloat16), "shard", scatter_dimension=axis, tiled=True
        )
        return lax.psum(part, "rep").astype(jnp.float32)

    square_dir, new_square_first, new_square_second = adam_update(
        total(partial, 0), square_first, square_second
    )
    narrow_dir, new_narrow_first, new_narrow_second = adam_update(
        total(narrow, 1), narrow_first, narrow_second
    )
    directions = lax.all_gather(square_dir.astype(jnp.bfloat16), "shard", axis=0, tiled=True)
    square_update = jnp.einsum(
        "imr,rin->imn", bases, directions, preferred_element_type=jnp.float32
    ).astype(jnp.bfloat16)
    narrow_update = lax.all_gather(narrow_dir.astype(jnp.bfloat16), "shard", axis=1, tiled=True)
    return (
        square_update,
        narrow_update,
        new_square_first,
        new_square_second,
        new_narrow_first,
        new_narrow_second,
    )


class Stream:
    def __init__(self, theirs, ours, refs):
        self.theirs, self.ours = theirs, ours
        (
            self.in1,
            self.sum1,
            self.in2,
            self.sum2,
            self.in3,
            self.total,
            self.direction,
            self.one,
            self.two,
            self.one_out,
            self.two_out,
            self.columns,
        ) = refs


def kernel(high, cuts, *refs):
    pieces = len(cuts)
    refs = list(refs)

    def take(number):
        taken = refs[:number]
        del refs[:number]
        return taken

    grads_hbm, narrow_hbm, bases_hbm, sq_one_hbm, sq_two_hbm, na_one_hbm, na_two_hbm = take(7)
    directions_out = take(pieces + 1)
    sq_one_out, sq_two_out, na_one_out, na_two_out = take(4)
    grads, bases, narrow, sq_one, sq_two, na_one, na_two = take(7)
    parts = take(pieces)
    buffers = [take(6) for _ in range(pieces + 1)]
    loads, sends, recvs = take(3)

    me_rep = lax.axis_index("rep")
    s = lax.axis_index("shard")
    c = lax.rem(me_rep, CORES)
    m = lax.rem(me_rep // CORES, MIDDLE)
    h = me_rep // (CORES * MIDDLE)

    def device(hh, mm, cc, ss):
        return ((hh * MIDDLE + mm) * CORES + cc, ss)

    def quad(ss, mm):
        return ss * MIDDLE + mm

    q = quad(s, m)
    core_peer = device(h, m, 1 - c, s)
    middle_peer = device(h, 1 - m, c, s)
    shard_peer = device(h, m, c, 1 - s)
    corner_peer = device(h, 1 - m, c, 1 - s)
    quad_peers = [
        (quad(1 - s, 1 - m), corner_peer),
        (quad(s, 1 - m), middle_peer),
        (quad(1 - s, m), shard_peer),
    ]
    high_peers = []
    for e in range(1, high):
        hh = lax.rem(h + e, high)
        high_peers.append((hh, device(hh, m, c, s)))

    barrier = pltpu.get_barrier_semaphore()
    everyone = [core_peer] + [peer for _, peer in high_peers + quad_peers]
    for peer in everyone:
        pl.semaphore_signal(barrier, inc=1, device_id=peer, device_id_type=MESH)

    loading = []

    def load(source, target):
        copy = pltpu.make_async_copy(source, target, loads.at[len(loading)])
        copy.start()
        loading.append(copy)
        return copy

    needed = {}

    half = grads.shape[1] // HALVES
    halves = [slice(k * half, (k + 1) * half) for k in range(HALVES)]

    def load_matrix(turn, i):
        needed[turn, "bases"] = load(bases_hbm.at[i], bases.at[i])
        for k, rows in enumerate(halves):
            needed[turn, k] = load(grads_hbm.at[i, rows], grads.at[i, rows])

    load_matrix(0, 1 - c)
    needed["narrow"] = load(narrow_hbm.at[c], narrow)
    moments = []

    def load_moments():
        moments.extend((load(na_one_hbm, na_one), load(na_two_hbm, na_two)))
        for i in range(CORES):
            moments.append(load(sq_one_hbm.at[:, i, :], sq_one.at[i]))
            moments.append(load(sq_two_hbm.at[:, i, :], sq_two.at[i]))

    waited = set()

    def ready(key):
        if key not in waited:
            waited.add(key)
            needed[key].wait()

    def moments_ready():
        while moments:
            moments.pop(0).wait()

    pending = []

    def remote(source, target, peer):
        at = len(pending)
        copy = pltpu.make_async_remote_copy(
            src_ref=source,
            dst_ref=target,
            send_sem=sends.at[at],
            recv_sem=recvs.at[at],
            device_id=peer,
            device_id_type=MESH,
        )
        pending.append(copy)
        return copy

    def send(source, target, peer):
        copy = remote(source, target, peer)
        copy.start()
        return copy

    def wide(value):
        return value.astype(jnp.float32)

    def adam(st, cc, mm, hh=None):
        where = (cc, mm) if hh is None else (cc, mm, hh)
        shape = st.total.shape[len(where) :]
        rows = math.prod(shape[:-1])
        first = mm * rows if hh is None else (mm * high + hh) * rows
        at = pl.ds(pl.multiple_of(first, 8), rows)
        gradient = wide(st.total[where]).reshape(rows, shape[-1])
        direction, one, two = adam_update(
            gradient, st.one[cc, at, st.columns], st.two[cc, at, st.columns]
        )
        st.direction[(cc, s) + where[1:]] = direction.astype(jnp.bfloat16).reshape(shape)
        st.one_out[cc, at, st.columns] = one
        st.two_out[cc, at, st.columns] = two

    def added(value, copies, arrivals):
        total = wide(value)
        for k, copy in enumerate(copies):
            copy.wait_recv()
            total = total + wide(arrivals[k])
        return total.astype(jnp.bfloat16)

    def core_sum(st):
        st.first.wait_recv()
        st.sum1[...] = (wide(st.ours[...]) + wide(st.in1[...])).astype(jnp.bfloat16)

    def quad_first(st):
        core_sum(st)
        second = [
            send(st.sum1.at[qq], st.in2.at[k], peer) for k, (qq, peer) in enumerate(quad_peers)
        ]
        yield
        st.sum2[...] = added(st.sum1[q], second, st.in2)
        third = [
            send(st.sum2.at[hh], st.in3.at[k], peer) for k, (hh, peer) in enumerate(high_peers)
        ]
        yield
        st.total[c, m, h] = added(st.sum2[h], third, st.in3)
        mine = st.total.at[c, m, h]
        back = [send(mine, mine, peer) for _, peer in high_peers]
        yield
        for copy in back:
            copy.wait_recv()
        mine = st.total.at[c, m]
        total_middle = send(mine, mine, middle_peer)
        moments_ready()
        adam(st, c, m)
        mine = st.direction.at[c, s, m]
        shard = send(mine, mine, shard_peer)
        corner = send(mine, mine, corner_peer)
        mine = st.total.at[c, m]
        last = [send(mine, mine, core_peer)]
        yield
        last.pop().wait_recv()
        adam(st, 1 - c, m)
        yield
        shard.wait_recv()
        came = st.direction.at[c, 1 - s, m]
        last.append(send(came, came, core_peer))
        yield
        total_middle.wait_recv()
        came = st.total.at[c, 1 - m]
        total_core = send(came, came, core_peer)
        adam(st, c, 1 - m)
        yield
        corner.wait_recv()
        came = st.direction.at[c, 1 - s, 1 - m]
        last.append(send(came, came, core_peer))
        yield
        total_core.wait_recv()
        adam(st, 1 - c, 1 - m)
        for copy in last:
            copy.wait_recv()

    def high_first(st):
        core_sum(st)
        second = [
            send(st.sum1.at[:, hh], st.in2.at[k], peer) for k, (hh, peer) in enumerate(high_peers)
        ]
        yield
        st.sum2[...] = added(st.sum1[:, h], second, st.in2)
        third = [
            send(st.sum2.at[qq], st.in3.at[k], peer) for k, (qq, peer) in enumerate(quad_peers)
        ]
        yield
        st.total[c, m, h] = added(st.sum2[q], third, st.in3)
        mine = st.total.at[c, m, h]
        back = [send(mine, mine, middle_peer)]
        moments_ready()
        adam(st, c, m, h)
        mine = st.direction.at[c, s, m, h]
        back.append(send(mine, mine, corner_peer))
        back.append(send(mine, mine, shard_peer))
        yield
        for copy in back:
            copy.wait_recv()
        totals, ours = st.total.at[c, :, h], st.direction.at[c, 1 - s, :, h]
        last = []
        for _, peer in high_peers:
            last.append(send(totals, totals, peer))
            last.append(send(ours, ours, peer))
        adam(st, c, 1 - m, h)
        yield
        for copy in last:
            copy.wait_recv()
        totals, ours = st.total.at[c], st.direction.at[c, 1 - s]
        total_core = send(totals, totals, core_peer)
        direction_core = send(ours, ours, core_peer)
        for hh, _ in high_peers:
            for mm in range(MIDDLE):
                adam(st, c, mm, hh)
        yield
        total_core.wait_recv()
        for mm in range(MIDDLE):
            adam(st, 1 - c, mm)
        direction_core.wait_recv()

    def project(turn, i):
        ready((turn, "bases"))
        part = None
        for k, rows in enumerate(halves):
            ready((turn, k))
            product = lax.dot_general(
                bases[i, rows],
                grads[i, rows],
                (((0,), (0,)), ((), ())),
                preferred_element_type=jnp.float32,
            )
            part = product if part is None else part + product
        for k, cut in enumerate(cuts):
            parts[k][i] = part[:, cut].astype(jnp.bfloat16).reshape(parts[k].shape[1:])

    streams = [
        Stream(
            narrow_hbm.at[1 - c],
            narrow,
            buffers[pieces]
            + [directions_out[pieces], na_one, na_two, na_one_out, na_two_out, slice(None)],
        )
    ]
    for k, cut in enumerate(cuts):
        streams.append(
            Stream(
                parts[k].at[1 - c],
                parts[k].at[c],
                buffers[k] + [directions_out[k], sq_one, sq_two, sq_one_out, sq_two_out, cut],
            )
        )
    for st in streams:
        st.first = remote(st.theirs, st.in1, core_peer)
    running = [high_first(streams[0])] + [quad_first(st) for st in streams[1:]]

    load_matrix(1, c)
    pl.semaphore_wait(barrier, len(everyone))
    streams[0].first.start()
    project(0, 1 - c)
    for st in streams[1:]:
        st.first.start()
    ready("narrow")
    next(running[0], None)
    project(1, c)
    load_moments()
    for at in sequence(pieces)[1:]:
        next(running[at], None)
    for copy in pending:
        copy.wait_send()


def sequence(pieces):
    square = list(range(1, pieces + 1))
    turns = [0] + square
    turns += square + [0]
    turns += square[:1] + [0] + square[1:]
    turns += square[:1] + [0] + square[1:]
    turns += square
    turns += square[:1] * 3 + [0]
    for k in square[1:]:
        turns += [k] * 3
    return turns + [0] + square


def finish(cuts, bases_ref, *refs):
    sq_dir_refs = refs[: len(cuts)]
    na_dir_ref, sq_one_ref, sq_two_ref, na_one_ref, na_two_ref = refs[len(cuts) : len(cuts) + 5]
    update_out, na_update_out, sq_one_out, sq_two_out, na_one_out, na_two_out = refs[-9:-3]
    update, sems, tile_sems = refs[-3:]
    pairs = [(na_dir_ref, na_update_out), (na_one_ref, na_one_out), (na_two_ref, na_two_out)]
    for i in range(CORES):
        pairs.append((sq_one_ref.at[i], sq_one_out.at[:, i, :]))
        pairs.append((sq_two_ref.at[i], sq_two_out.at[:, i, :]))
    copies = [
        pltpu.make_async_copy(source, target, sems.at[k])
        for k, (source, target) in enumerate(pairs)
    ]
    for copy in copies:
        copy.start()
    height = update.shape[1] // TILES
    for i in range(CORES):
        for t in range(TILES):
            rows = pl.ds(t * height, height)
            for cut, sq_dir_ref in zip(cuts, sq_dir_refs):
                update[i, rows, cut] = jnp.dot(
                    bases_ref[i, rows], sq_dir_ref[i], preferred_element_type=jnp.float32
                ).astype(jnp.bfloat16)
            copy = pltpu.make_async_copy(
                update.at[i, rows], update_out.at[i, rows], tile_sems.at[i, t]
            )
            copy.start()
            copies.append(copy)
    for copy in copies:
        copy.wait()


def kernel_exchange(reps, square, narrow, bases, square_first, square_second, narrow_first, narrow_second):
    matrices, width, columns = square.shape
    rank = bases.shape[2]
    high = reps // (CORES * MIDDLE)
    shards = SHARDS
    quads = shards * MIDDLE
    bf16, f32 = jnp.bfloat16, jnp.float32
    cuts = []
    while sum(cut.stop - cut.start for cut in cuts) < columns:
        begin = cuts[-1].stop if cuts else 0
        size = -(-(columns - begin) // ((PIECES - len(cuts)) * 128)) * 128
        cuts.append(slice(begin, min(columns, begin + size)))
    kinds = [(rank // (quads * high), cut.stop - cut.start) for cut in cuts]
    na = (width // (quads * high), narrow.shape[2])
    kinds.append(na)
    own = (matrices, MIDDLE, high)
    own_square = (matrices, rank // shards, columns)

    buffers = []
    for kind in kinds:
        inner, outer = (quads, high) if kind is na else (high, quads)
        shapes = [
            (quads, high) + kind,
            (quads, high) + kind,
            (outer - 1, inner) + kind,
            (inner,) + kind,
            (inner - 1,) + kind,
            own + kind,
        ]
        buffers += [pltpu.VMEM(shape, bf16) for shape in shapes]
    copies = len(kinds) * (8 + (quads - 1) + 4 * (high - 1))
    vmem = pl.BlockSpec(memory_space=pltpu.VMEM)
    anywhere = pl.BlockSpec(memory_space=pl.ANY)
    out = pl.pallas_call(
        functools.partial(kernel, high, cuts),
        out_shape=tuple(
            [jax.ShapeDtypeStruct((matrices, shards, MIDDLE, high) + kind, bf16) for kind in kinds]
            + [jax.ShapeDtypeStruct(own_square, f32)] * 2
            + [jax.ShapeDtypeStruct(narrow_first.shape, f32)] * 2
        ),
        in_specs=[pl.BlockSpec(memory_space=pltpu.HBM)] * 7,
        out_specs=[vmem] * (len(kinds) + 4),
        scratch_shapes=[
            pltpu.VMEM(square.shape, bf16),
            pltpu.VMEM(bases.shape, bf16),
            pltpu.VMEM((quads, high) + na, bf16),
            pltpu.VMEM(own_square, f32),
            pltpu.VMEM(own_square, f32),
            pltpu.VMEM(narrow_first.shape, f32),
            pltpu.VMEM(narrow_first.shape, f32),
        ]
        + [pltpu.VMEM((matrices, quads, high) + kind, bf16) for kind in kinds[:-1]]
        + buffers
        + [
            pltpu.SemaphoreType.DMA((2 * (1 + HALVES) + 3 + 2 * matrices,)),
            pltpu.SemaphoreType.DMA((copies,)),
            pltpu.SemaphoreType.DMA((copies,)),
        ],
        compiler_params=pltpu.CompilerParams(
            collective_id=0, has_side_effects=True, vmem_limit_bytes=48 * 1024 * 1024
        ),
        name="galore_exchange",
    )(
        *[
            pltpu.with_memory_space_constraint(operand, pltpu.HBM)
            for operand in (
                square,
                narrow.reshape((matrices, quads, high) + na),
                bases,
                square_first,
                square_second,
                narrow_first,
                narrow_second,
            )
        ]
    )
    *sq_dirs, na_dir, sq_one, sq_two, na_one, na_two = out
    return pl.pallas_call(
        functools.partial(finish, cuts),
        out_shape=(
            jax.ShapeDtypeStruct(square.shape, bf16),
            jax.ShapeDtypeStruct(narrow.shape, bf16),
            jax.ShapeDtypeStruct(square_first.shape, f32),
            jax.ShapeDtypeStruct(square_second.shape, f32),
            jax.ShapeDtypeStruct(narrow_first.shape, f32),
            jax.ShapeDtypeStruct(narrow_second.shape, f32),
        ),
        in_specs=[vmem] * (6 + len(cuts)),
        out_specs=[anywhere] * 6,
        scratch_shapes=[
            pltpu.VMEM(square.shape, bf16),
            pltpu.SemaphoreType.DMA((7,)),
            pltpu.SemaphoreType.DMA((matrices, TILES)),
        ],
        compiler_params=pltpu.CompilerParams(vmem_limit_bytes=24 * 1024 * 1024),
        name="galore_finish",
    )(
        bases,
        *[part.reshape(matrices, rank, -1) for part in sq_dirs],
        na_dir.reshape(narrow.shape),
        sq_one,
        sq_two,
        na_one,
        na_two,
    )


def on_device(square_grads, narrow_grads, galore_bases, *moments):
    shards, reps = lax.axis_size("shard"), lax.axis_size("rep")
    square, narrow = square_grads[0, 0], narrow_grads[0, 0]
    chunks = shards * reps // CORES
    fits = (
        reps % (CORES * MIDDLE) == 0
        and reps > CORES * MIDDLE
        and shards == SHARDS
        and square.shape[0] == CORES
        and square.shape[2] % 128 == 0
        and square.shape[2] >= PIECES * 128
        and galore_bases.shape[2] % (16 * chunks) == 0
        and square.shape[1] % (8 * chunks) == 0
        and square.shape[1] % (16 * TILES) == 0
    )
    run = functools.partial(kernel_exchange, reps) if fits else plain_exchange
    return run(square, narrow, galore_bases, *moments)


def solution(mesh):
    placed = (
        P("rep", "shard", None, None, None),
        P("rep", "shard", None, None, None),
        P(),
        P("shard", None, None),
        P("shard", None, None),
        P(None, "shard", None),
        P(None, "shard", None),
    )
    return jax.shard_map(
        on_device,
        mesh=mesh,
        in_specs=placed,
        out_specs=(
            P(),
            P(),
            P("shard", None, None),
            P("shard", None, None),
            P(None, "shard", None),
            P(None, "shard", None),
        ),
        check_vma=False,
    )
```
